32 devices in a mesh: tile: 8 (over z, y), head: 4 (over x, core).
Axes of the slice: x: 2, y: 2, z: 4, core: 2. Of those that a mesh axis runs over, the one named last changes fastest.
Arguments:
- tokens: bfloat16 [256, 32768], P('head', 'tile'), may hold values from -6 to 6
- grad_in: bfloat16 [256, 32768], P('head', 'tile'), may hold values from -6 to 6
- w_qkv: bfloat16 [3, 256, 256], P(None, 'head'), may hold values from -0.375 to 0.375
- w_out: bfloat16 [256, 256], P('head'), may hold values from -0.375 to 0.375
- neighbors: int32 [9, 32768], P(None, 'tile'), may hold values from 0 to 4479, as said below
- send_rows: int32 [8, 3, 128], P('tile'), may hold values from 0 to 4096, as said below
Outputs:
- d_tokens: float32 [256, 32768], P('head', 'tile')
- grad_qkv: float32 [3, 256, 256], P(None, 'head')
- grad_out: float32 [256, 256], P('head')
The draws below stay inside these ranges and needn't reach their ends.
Inputs may be any that keep to these rules, and one draw needn't show every extreme that they name: `send_rows`: entries of list p of index d are rows of index d, live entries first, the rest equal to 4096; list 2 of every index is full, and list 0 of index 0 is half full. `neighbors`: slot 0 of row r of an index is r itself; an entry below 4096 lies within 64 rows of r, counted around the index's 4096 rows; every entry at or above 4096 points to a live entry of the list it names.
All inputs are finite; a program needn't handle non-finite values.
Results may differ from the reference program's by a relative error of at most 0.0059.
Values may be sent and summed in bfloat16 or wider, within the bound.
A program may use at most 64 MiB of HBM per device.

```python
import math
import jax
import jax.numpy as jnp
from jax import lax

C = 256
HEADS = 8
NBR = 9
ROWS_DEV = 4096
BORDER = 128
GROUPS = 8
ROWS = 32768


def border_counts(key):
    counts = jax.random.randint(jax.random.fold_in(key, 11), (GROUPS, 3), BORDER // 2, BORDER + 1)
    counts = counts.at[:, 2].set(BORDER)
    counts = counts.at[0, 0].set(BORDER // 2)
    return counts.astype(jnp.int32)


def draw_send_rows(key, part):
    counts = border_counts(key)
    subkeys = jax.random.split(jax.random.fold_in(key, 23), GROUPS * 3)
    chosen = jax.vmap(lambda subkey: jax.random.permutation(subkey, ROWS_DEV)[:BORDER])(subkeys)
    chosen = chosen.reshape(GROUPS, 3, BORDER)
    column = jnp.arange(BORDER, dtype=jnp.int32)
    return jnp.where(column[None, None, :] < counts[:, :, None], chosen, ROWS_DEV).astype(jnp.int32)


def draw_neighbors(key, part):
    counts = border_counts(key)
    first, second, third, fourth = jax.random.split(jax.random.fold_in(key, 37), 4)
    shape = (NBR - 1, GROUPS, ROWS_DEV)
    row_ids = jnp.arange(ROWS_DEV, dtype=jnp.int32)
    local = (row_ids[None, None, :] + jax.random.randint(first, shape, -64, 65)) % ROWS_DEV
    peer = jax.random.randint(second, shape, 0, 3)
    device = jnp.arange(GROUPS, dtype=jnp.int32)[None, :, None]
    offsets = jnp.array([1, GROUPS - 1, GROUPS // 2], dtype=jnp.int32)
    source = (device - offsets[peer]) % GROUPS
    live = counts[source, peer]
    column = jax.random.randint(third, shape, 0, BORDER) % live
    remote = ROWS_DEV + peer * BORDER + column
    picked = jax.random.randint(fourth, shape, 0, 8) == 0
    entries = jnp.where(picked, remote, local)
    entries = entries.at[NBR - 2, :, 0].set(ROWS_DEV + 3 * BORDER - 1)
    selfrow = jnp.broadcast_to(row_ids[None, None, :], (1, GROUPS, ROWS_DEV))
    whole = jnp.concatenate([selfrow, entries], axis=0)
    return whole.reshape(NBR, GROUPS * ROWS_DEV).astype(jnp.int32)


def block_levels(stream_key, extent, pieces, low, largest):
    loudness, own = 1.0, jax.random.fold_in(stream_key, 6)
    for dim, parts in pieces:
        heights = jnp.exp(jax.random.uniform(jax.random.fold_in(own, dim), (parts,), jnp.float32, low / len(pieces), largest / len(pieces)))
        loudness = loudness * jnp.repeat(heights, extent[dim] // parts).reshape([-1 if axis == dim else 1 for axis in range(len(extent))])
    return loudness


def gaussian(stream_key, shape, width, limit, shards=(), kind=jnp.bfloat16):
    level = block_levels(stream_key, shape, shards, -0.22, 0.18) if shards else 1.0
    values = jax.random.normal(stream_key, shape, jnp.float32) * width * level
    return jnp.minimum(jnp.maximum(values, -limit), limit).astype(kind)


def setup_inputs(seed: int = 0) -> dict:
    streams_of = jax.random.split(jax.random.key(seed), 7)
    return {
        "tokens": gaussian(streams_of[0], (C, ROWS), 1.0, 6.0, ((0, 4), (1, 8))),
        "grad_in": gaussian(streams_of[1], (C, ROWS), 1.0, 6.0, ((0, 4), (1, 8))),
        "w_qkv": gaussian(streams_of[2], (3, C, C), C ** -0.5, 0.375, ((1, 4),)),
        "w_out": gaussian(streams_of[3], (C, C), C ** -0.5, 0.375, ((0, 4),)),
        "neighbors": draw_neighbors(jax.random.fold_in(streams_of[6], 71), 0),
        "send_rows": draw_send_rows(jax.random.fold_in(streams_of[6], 71), 0),
    }


def reference(tokens, grad_in, w_qkv, w_out, neighbors, send_rows):
    total_rows = GROUPS * ROWS_DEV
    head_dim = C // HEADS
    score_scale = 1.0 / math.sqrt(head_dim)
    devices = jnp.arange(GROUPS, dtype=jnp.int32)
    offsets = jnp.array([1, GROUPS - 1, GROUPS // 2], dtype=jnp.int32)
    sources = (devices[:, None] - offsets[None, :]) % GROUPS
    lists = send_rows[sources, jnp.arange(3, dtype=jnp.int32)[None, :], :]
    remote = jnp.where(lists < ROWS_DEV, sources[:, :, None] * ROWS_DEV + lists, total_rows).astype(jnp.int32)
    own_rows = devices[:, None] * ROWS_DEV + jnp.arange(ROWS_DEV, dtype=jnp.int32)[None, :]
    mapping = jnp.concatenate([own_rows, remote.reshape(GROUPS, 3 * BORDER)], axis=1)
    local_table = neighbors.reshape(NBR, GROUPS, ROWS_DEV)
    table = mapping[devices[None, :, None], local_table].reshape(NBR, total_rows).astype(jnp.int32)
    x_rows = tokens.T
    dy_rows = grad_in.T
    query = jnp.dot(x_rows, w_qkv[0].T, preferred_element_type=jnp.float32).astype(jnp.bfloat16)
    keys = jnp.dot(x_rows, w_qkv[1].T, preferred_element_type=jnp.float32).astype(jnp.bfloat16)
    values = jnp.dot(x_rows, w_qkv[2].T, preferred_element_type=jnp.float32).astype(jnp.bfloat16)
    packed = jnp.concatenate([keys, values], axis=1)
    padded = jnp.concatenate([packed, jnp.zeros((1, 2 * C), jnp.bfloat16)], axis=0)
    grad_att = jnp.dot(dy_rows, w_out.T, preferred_element_type=jnp.float32)

    def block_step(totals, block_index):
        start = (block_index * ROWS_DEV).astype(jnp.int32)
        picks = lax.dynamic_slice_in_dim(table, start, ROWS_DEV, 1)
        near = padded[picks].astype(jnp.float32)
        near_keys = near[:, :, :C].reshape(NBR, ROWS_DEV, HEADS, head_dim)
        near_values = near[:, :, C:].reshape(NBR, ROWS_DEV, HEADS, head_dim)
        query_rows = lax.dynamic_slice_in_dim(query, start, ROWS_DEV, 0).astype(jnp.float32).reshape(ROWS_DEV, HEADS, head_dim)
        dout_rows = lax.dynamic_slice_in_dim(grad_att, start, ROWS_DEV, 0).reshape(ROWS_DEV, HEADS, head_dim)
        scores = jnp.einsum('rhd,jrhd->jrh', query_rows, near_keys) * score_scale
        expon = jnp.exp(scores)
        probs = expon / lax.optimization_barrier(jnp.sum(expon, axis=0))
        attended = jnp.einsum('jrh,jrhd->rhd', probs, near_values)
        dprob = jnp.einsum('rhd,jrhd->jrh', dout_rows, near_values)
        dscore = probs * (dprob - lax.optimization_barrier(jnp.sum(probs * dprob, axis=0)))
        grad_query = jnp.einsum('jrh,jrhd->rhd', dscore, near_keys) * score_scale
        grad_keys = dscore[..., None] * query_rows[None] * score_scale
        grad_values = probs[..., None] * dout_rows[None]
        grad_near = jnp.concatenate([grad_keys.reshape(NBR, ROWS_DEV, C), grad_values.reshape(NBR, ROWS_DEV, C)], axis=2)
        totals = totals.at[picks.reshape(-1)].add(grad_near.reshape(NBR * ROWS_DEV, 2 * C))
        return (totals, (attended.reshape(ROWS_DEV, C).astype(jnp.bfloat16), grad_query.reshape(ROWS_DEV, C)))
    totals, (attended, grad_query) = lax.scan(block_step, jnp.zeros((total_rows + 1, 2 * C), jnp.float32), jnp.arange(GROUPS, dtype=jnp.int32))
    attended = attended.reshape(total_rows, C)
    grad_q = grad_query.reshape(total_rows, C).astype(jnp.bfloat16)
    grad_k = totals[:total_rows, :C].astype(jnp.bfloat16)
    grad_v = totals[:total_rows, C:].astype(jnp.bfloat16)
    d_rows = dy_rows.astype(jnp.float32) + jnp.dot(grad_q, w_qkv[0], preferred_element_type=jnp.float32) + jnp.dot(grad_k, w_qkv[1], preferred_element_type=jnp.float32) + jnp.dot(grad_v, w_qkv[2], preferred_element_type=jnp.float32)
    grad_scale = 1.0 / math.sqrt(total_rows)
    grad_qkv = jnp.stack([jnp.dot(grad_q.T, x_rows, preferred_element_type=jnp.float32), jnp.dot(grad_k.T, x_rows, preferred_element_type=jnp.float32), jnp.dot(grad_v.T, x_rows, preferred_element_type=jnp.float32)]) * grad_scale
    grad_out = jnp.dot(attended.T, dy_rows, preferred_element_type=jnp.float32) * grad_scale
    return (d_rows.T, grad_qkv, grad_out)
```

```python
import functools
import math

import jax
import jax.numpy as jnp
from jax import lax
from jax.experimental import pallas as pl
from jax.experimental.pallas import tpu as pltpu
from jax.sharding import PartitionSpec as P

C = 256
HEADS = 8
NBR = 9
MARGIN = 64
BLOCK = 2 * MARGIN
WINDOW = 2 * BLOCK
CHUNK = 2 * BLOCK
NEVER = -1.0e30

NN = (((1,), (0,)), ((), ()))
NT = (((1,), (1,)), ((), ()))


def mm(a, b, dims=NN):
    return lax.dot_general(a, b, dims, preferred_element_type=jnp.float32)


def on_mesh(tile, head):
    return {"tile": tile, "head": head}


def greet(peers):
    barrier = pltpu.get_barrier_semaphore()
    for peer in peers:
        pl.semaphore_signal(barrier, inc=1, device_id=peer, device_id_type=pl.DeviceIdType.MESH)
    pl.semaphore_wait(barrier, len(peers))


def remote(src, dst, send_sem, recv_sem, peer):
    return pltpu.make_async_remote_copy(
        src_ref=src,
        dst_ref=dst,
        send_sem=send_sem,
        recv_sem=recv_sem,
        device_id=peer,
        device_id_type=pl.DeviceIdType.MESH,
    )


def send(*args):
    copy = remote(*args)
    copy.start()
    return copy


def attention_body(
    groups, heads, share, border, rows, grad_scale,
    tokens, grad_in, w_qkv, w_out, neighbors, send_rows,
    d_out, gqkv_out, gout_out,
    tok, dy, xr, yr, wr, wkd, wvp, wt, chosen, mine, bias_s, twice,
    k_s, v_s, kt_s, vt_s, qaug, qdiag, gdiag, e_s, p_s, ds_s,
    gk_s, gv_s, att_s, gq_s, dw, dwo, pr, fr, s1, rs, totals,
    dout, bk, db, answers, result,
    local_sem, w_send, w_recv, wf_send, wf_recv, xp_send, xp_recv, yp_send, yp_recv,
    x_send, x_recv, y_send, y_recv, e_send, e_recv, ef_send, ef_recv,
    d_send, d_recv, b_send, b_recv, p_send, p_recv, f_send, f_recv,
    r_send, r_recv, g_send, g_recv, out_sem,
):
    head_dim = C // HEADS
    wide_head = 2 * head_dim
    pairs = HEADS // 2
    scale = 1.0 / math.sqrt(head_dim)
    scale2 = scale / math.log(2.0)
    near = rows + BLOCK
    keys = near + 3 * border
    wide = WINDOW + 3 * border
    tiles = wide // BLOCK
    full_rows = rows * heads
    chunks = rows // CHUNK
    bf16, f32 = jnp.bfloat16, jnp.float32
    tile, me = lax.axis_index("tile"), lax.axis_index("head")
    offsets = (1, groups - 1, groups // 2)
    partner = (me // 2) * 2 + 1 - me % 2
    steps = range(2, heads, 2)
    others = [(me + k) % heads for k in range(1, heads)]
    peers = [(tile + k) % groups for k in range(1, groups)]

    def rows_of(index):
        return pl.ds(pl.multiple_of(index * share, share), share)

    def lanes(start, size):
        return pl.ds(pl.multiple_of(start, BLOCK), size)

    greet(
        [on_mesh(tile, to) for to in others]
        + [on_mesh(to, me) for to in peers]
        + [on_mesh((tile + offset) % groups, to) for offset in offsets for to in others]
    )

    locals_ = [pltpu.make_async_copy(tokens, tok, local_sem.at[0])]
    pairs_of = ((tokens, xr), (grad_in, yr))
    own = lanes(me * rows, rows)
    after = lanes(((me + 1) % heads) * rows, BLOCK)
    for i, (src, dst) in enumerate(pairs_of):
        locals_.append(pltpu.make_async_copy(src.at[:, own], dst.at[rows_of(me), 0:rows], local_sem.at[1 + 2 * i]))
        locals_.append(
            pltpu.make_async_copy(src.at[:, after], dst.at[rows_of(me), rows:near], local_sem.at[2 + 2 * i])
        )
    locals_.append(pltpu.make_async_copy(w_qkv, wr.at[0:3, rows_of(me), :], local_sem.at[5]))
    locals_.append(pltpu.make_async_copy(w_out, wr.at[3, rows_of(me), :], local_sem.at[6]))
    locals_.append(pltpu.make_async_copy(grad_in, dy, local_sem.at[7]))
    for copy in locals_:
        copy.start()

    w_copies = []
    for i, to in enumerate([(me + k) % heads for k in steps] + [partner]):
        w_copies.append(
            [
                send(w_qkv, wr.at[0:3, rows_of(me), :], w_send.at[0, i], w_recv.at[0, i], on_mesh(tile, to)),
                send(w_out, wr.at[3, rows_of(me), :], w_send.at[1, i], w_recv.at[1, i], on_mesh(tile, to)),
            ]
        )
    moving = []
    for i, to in enumerate(others):
        for src, dst, ss, rr in ((tokens, xr, xp_send, xp_recv), (grad_in, yr, yp_send, yp_recv)):
            moving.append(
                send(src.at[:, lanes(to * rows, BLOCK)], dst.at[rows_of(me), 0:BLOCK], ss.at[i], rr.at[i], on_mesh(tile, to))
            )

    def piece(c):
        return lanes(BLOCK + c * CHUNK, CHUNK)

    def send_chunk(c):
        for i, to in enumerate(others):
            for src, dst, ss, rr in ((tokens, xr, x_send, x_recv), (grad_in, yr, y_send, y_recv)):
                first = BLOCK + c * CHUNK
                if c < chunks - 1:
                    parts = ((first, to * rows + first, CHUNK),)
                else:
                    parts = (
                        (first, to * rows + first, BLOCK),
                        (rows, ((to + 1) % heads) * rows, BLOCK),
                    )
                for at, frm, size in parts:
                    send(
                        src.at[:, lanes(frm, size)], dst.at[rows_of(me), at : at + size],
                        ss.at[i, c], rr.at[i, c], on_mesh(tile, to),
                    )

    def chunk_copies(c):
        copies = []
        for i, to in enumerate(others):
            for src, dst, ss, rr in ((tokens, xr, x_send, x_recv), (grad_in, yr, y_send, y_recv)):
                copies.append(
                    remote(
                        src.at[:, 0:CHUNK], dst.at[rows_of(me), piece(c)],
                        ss.at[i, c], rr.at[i, c], on_mesh(tile, to),
                    )
                )
        return copies

    send_chunk(0)

    flat = jnp.concatenate([send_rows[0, p : p + 1, :] for p in range(3)], axis=1)

    def choose(i, carry):
        ids = lax.broadcasted_iota(jnp.int32, (CHUNK, 3 * border), 0) + i * CHUNK
        at = pl.ds(pl.multiple_of(i * CHUNK, CHUNK), CHUNK)
        chosen[at, :] = jnp.where(ids == flat, 1.0, 0.0).astype(bf16)
        return carry

    lax.fori_loop(0, full_rows // CHUNK, choose, 0)
    locals_[0].wait()
    mine[...] = mm(tok[...], chosen[...]).astype(bf16)
    e_copies = []
    for p in range(3):
        there = (tile + offsets[p]) % groups
        cols = slice(near + p * border, near + (p + 1) * border)
        for i, to in enumerate([(me + k) % heads for k in steps] + [me, partner]):
            e_copies.append(
                send(
                    mine.at[:, p * border : (p + 1) * border], xr.at[rows_of(me), cols],
                    e_send.at[p, i], e_recv.at[p, i], on_mesh(there, to),
                )
            )
    for c in range(1, chunks):
        send_chunk(c)

    def mask(b, carry):
        start = pl.multiple_of(b * BLOCK, BLOCK)
        here = me * rows + start
        one = neighbors[:, lanes(here, BLOCK)]
        two = neighbors[:, lanes((here + BLOCK) % full_rows, BLOCK)]
        ring = jnp.concatenate([one[:, MARGIN:], two[:, :MARGIN]], axis=1)
        along = ring - me * rows
        along = jnp.where(along < 0, along + full_rows, along)
        picks = jnp.where(ring < full_rows, along - start, ring - full_rows + WINDOW)
        for t in range(tiles):
            ids = lax.broadcasted_iota(jnp.int32, (BLOCK, BLOCK), 0) + t * BLOCK
            count = jnp.zeros((BLOCK, BLOCK), f32)
            for j in range(NBR):
                count = count + jnp.where(ids == picks[j : j + 1, :], 1.0, 0.0)
            bias = jnp.where(count > 0.0, jnp.log2(jnp.maximum(count, 1.0)), NEVER)
            bias_s[pl.ds(pl.multiple_of(b * wide + t * BLOCK, BLOCK), BLOCK), :] = bias.astype(bf16)
        return carry

    lax.fori_loop(0, rows // BLOCK, mask, 0)
    qaug[...] = jnp.zeros_like(qaug)
    qdiag[...] = jnp.zeros_like(qdiag)
    gdiag[...] = jnp.zeros_like(gdiag)
    gk_s[...] = jnp.zeros_like(gk_s)
    gv_s[...] = jnp.zeros_like(gv_s)
    dw[...] = jnp.zeros_like(dw)
    for ref in (att_s, gq_s):
        ref[:, :BLOCK] = jnp.zeros((C, BLOCK), f32)
        ref[:, near:] = jnp.zeros((C, BLOCK), f32)
    diag = jnp.where(
        lax.broadcasted_iota(jnp.int32, (BLOCK, BLOCK), 0) == lax.broadcasted_iota(jnp.int32, (BLOCK, BLOCK), 1), 1.0, 0.0
    ).astype(bf16)
    twice[:, :BLOCK] = diag
    twice[:, BLOCK:] = diag
    wvp[...] = jnp.zeros_like(wvp)

    last = []
    for i, k in enumerate(steps):
        for copy in w_copies[i]:
            copy.wait()
        block_ref = wr.at[:, rows_of((me + heads - k) % heads), :]
        last.append(send(block_ref, block_ref, wf_send.at[i], wf_recv.at[i], on_mesh(tile, partner)))
    for copy in w_copies[len(steps)]:
        copy.wait()
    for copy in e_copies:
        copy.wait()
    for i, k in enumerate(steps):
        block_ref = xr.at[rows_of((me + heads - k) % heads), near:keys]
        last.append(send(block_ref, block_ref, ef_send.at[i], ef_recv.at[i], on_mesh(tile, partner)))
    for copy in locals_[1:]:
        copy.wait()
    for i in range(len(steps)):
        last[i].wait()
    for t in range(3):
        wt[t] = wr[t].T
    for pair in range(pairs):
        chan = slice(pair * wide_head, (pair + 1) * wide_head)
        base = pair * 2 * wide_head
        wkd[base : base + wide_head, :] = wr[1, chan, :]
        wkd[base + wide_head : base + 2 * wide_head, :] = wr[1, chan, :]
        wvp[base : base + wide_head, :] = wr[2, chan, :]

    lane_id = lax.broadcasted_iota(jnp.int32, (1, 2 * C), 1) % (2 * wide_head)
    ones = jnp.where((lane_id >= wide_head) & (lane_id < wide_head + 3), 1.0, 0.0)

    def project(at_rows, at_cols):
        x = xr[:, at_cols]
        xt = x.T
        k_s[at_rows, :] = mm(xt, wkd[...], NT).astype(bf16)
        v_s[at_rows, :] = (mm(xt, wvp[...], NT) + ones).astype(bf16)
        kt_s[:, at_cols] = mm(wr[1], x).astype(bf16)
        vt_s[:, at_cols] = mm(wr[2], x).astype(bf16)

    for copy in moving:
        copy.wait()
    project(slice(0, BLOCK), slice(0, BLOCK))
    for i in range(len(steps)):
        last[len(steps) + i].wait()
    project(slice(near, keys), slice(near, keys))

    def gradients(cols, size):
        around = lanes(cols, size + BLOCK)
        gq = pltpu.roll(gq_s[:, around], size + MARGIN, 1)[:, :size].astype(bf16)
        att = pltpu.roll(att_s[:, around], size + MARGIN, 1)[:, :size].astype(bf16)
        here = lanes(cols, size)
        gk = (gk_s[:, here] * scale).astype(bf16)
        gv = gv_s[:, here].astype(bf16)
        x = xr[:, here]
        for t, (left, right) in enumerate(((gq, x), (gk, x), (gv, x), (att, yr[:, here]))):
            dw[:, t * C : (t + 1) * C] += mm(left, right, NT)
        d = mm(wt[0], gq) + mm(wt[1], gk) + mm(wt[2], gv)
        dout[:, here] = d.astype(bf16)
        bk[me, :, here] = dout[rows_of(me), here]

    def d_copies(cols, size, c):
        return [
            remote(
                dout.at[rows_of(to), lanes(cols, size)], bk.at[me, :, lanes(cols, size)],
                d_send.at[i, c], d_recv.at[i, c], on_mesh(tile, to),
            )
            for i, to in enumerate(others)
        ]

    def chunk(c, carry):
        base = pl.multiple_of(c * CHUNK, CHUNK)
        for copy in chunk_copies(c):
            copy.wait()
        project(pl.ds(pl.multiple_of(base + BLOCK, BLOCK), CHUNK), piece(c))
        around = lanes(base, CHUNK + BLOCK)
        q = pltpu.roll(mm(wr[0], xr[:, around]), CHUNK + MARGIN, 1)[:, :CHUNK].astype(bf16)
        g = pltpu.roll(mm(wr[3], yr[:, around]), CHUNK + MARGIN, 1)[:, :CHUNK].astype(bf16)
        scaled = q.astype(f32) * scale2
        high = scaled.astype(bf16)
        low = (scaled - high.astype(f32)).astype(bf16)
        for half in range(2):
            cols = slice(half * BLOCK, (half + 1) * BLOCK)
            for pair in range(pairs):
                u = half * pairs + pair
                for side in range(2):
                    chan = slice((pair * 2 + side) * head_dim, (pair * 2 + side + 1) * head_dim)
                    at = slice(side * head_dim, (side + 1) * head_dim)
                    under = slice(wide_head + side * head_dim, wide_head + (side + 1) * head_dim)
                    lane = slice(side * BLOCK, (side + 1) * BLOCK)
                    qaug[u, at, lane] = high[chan, cols]
                    qaug[u, under, lane] = low[chan, cols]
                    qdiag[u, at, lane] = q[chan, cols]
                    gdiag[u, at, lane] = g[chan, cols]

        units = 2 * pairs
        total, inv, right = {}, {}, {}

        def place(u):
            half, pair = u // pairs, u % pairs
            start = pl.multiple_of(base + half * BLOCK, BLOCK)
            return start, pair, slice(pair * wide_head, (pair + 1) * wide_head)

        def key_rows(u, t):
            start = place(u)[0]
            if t < WINDOW // BLOCK:
                return pl.ds(pl.multiple_of(start + t * BLOCK, BLOCK), BLOCK)
            first = near + t * BLOCK - WINDOW
            return slice(first, first + BLOCK)

        def score(u, t):
            pair = u % pairs
            if t == 0:
                total[u] = jnp.zeros((8, 2 * BLOCK), f32)
            at = slice(t * BLOCK, (t + 1) * BLOCK)
            row = (c * 2 + u // pairs) * wide + t * BLOCK
            left = jnp.concatenate(
                [
                    k_s[key_rows(u, t), pair * BLOCK : (pair + 1) * BLOCK],
                    bias_s[pl.ds(pl.multiple_of(row, BLOCK), BLOCK), :],
                ],
                axis=1,
            )
            e = jnp.exp2(mm(left, jnp.concatenate([qaug[u], twice[...]], axis=0)))
            total[u] = total[u] + jnp.sum(e.reshape(BLOCK // 8, 8, 2 * BLOCK), axis=0)
            e_s[u % 2, at, :] = e

        def normal(u, t):
            if t == 0:
                inv[u] = 1.0 / jnp.sum(total[u], axis=0, keepdims=True)
            at = slice(t * BLOCK, (t + 1) * BLOCK)
            p = e_s[u % 2, at, :] * inv[u]
            e_s[u % 2, at, :] = p
            p_s[u % 2, at, :] = p.astype(bf16)

        def spans(u):
            return (lanes(place(u)[0], WINDOW), slice(0, WINDOW)), (slice(near, keys), slice(WINDOW, wide))

        def attend(u):
            start, pair, chan = place(u)
            att = jnp.zeros((wide_head, 2 * BLOCK), f32)
            for span, at in spans(u):
                att = att + mm(vt_s[chan, span], p_s[u % 2, at, :])
            gd = gdiag[u]
            mean = -jnp.sum(att * gd.astype(f32), axis=0, keepdims=True)
            m0 = mean.astype(bf16).astype(f32)
            m1 = (mean - m0).astype(bf16).astype(f32)
            m2 = mean - m0 - m1
            ids = lax.broadcasted_iota(jnp.int32, (16, 2 * BLOCK), 0)
            rows3 = jnp.where(ids == 0, m0, jnp.where(ids == 1, m1, jnp.where(ids == 2, m2, 0.0))).astype(bf16)
            right[u] = jnp.concatenate([gd, rows3, jnp.zeros((wide_head - 16, 2 * BLOCK), bf16)], axis=0)
            cols = lanes(start + BLOCK, BLOCK)
            first = pair * wide_head
            att_s[first : first + head_dim, cols] = att[:head_dim, :BLOCK]
            att_s[first + head_dim : first + wide_head, cols] = att[head_dim:, BLOCK:]

        def value_grad(u):
            _, _, chan = place(u)
            for span, at in spans(u):
                gv_s[chan, span] += mm(gdiag[u], p_s[u % 2, at, :], NT)

        def dscore(u, t):
            pair = u % pairs
            at = slice(t * BLOCK, (t + 1) * BLOCK)
            dp = mm(v_s[key_rows(u, t), pair * BLOCK : (pair + 1) * BLOCK], right[u])
            ds_s[u % 2, at, :] = (e_s[u % 2, at, :] * dp).astype(bf16)

        def query_grad(u):
            start, pair, chan = place(u)
            gq = jnp.zeros((wide_head, 2 * BLOCK), f32)
            for span, at in spans(u):
                gq = gq + mm(kt_s[chan, span], ds_s[u % 2, at, :])
            gq = gq * scale
            cols = lanes(start + BLOCK, BLOCK)
            first = pair * wide_head
            gq_s[first : first + head_dim, cols] = gq[:head_dim, :BLOCK]
            gq_s[first + head_dim : first + wide_head, cols] = gq[head_dim:, BLOCK:]

        def key_grad(u):
            _, _, chan = place(u)
            for span, at in spans(u):
                gk_s[chan, span] += mm(qdiag[u], ds_s[u % 2, at, :], NT)

        for u in range(units + 1):
            for t in range(tiles):
                if u < units:
                    score(u, t)
                if u > 0:
                    dscore(u - 1, t)
            for t in range(tiles):
                if u < units:
                    normal(u, t)
                if u > 0 and t == 1:
                    query_grad(u - 1)
                if u > 0 and t == 3:
                    key_grad(u - 1)
            if u < units:
                attend(u)
                value_grad(u)

        gradients(base, CHUNK)
        for copy in d_copies(base, CHUNK, c):
            copy.start()
        return carry

    lax.fori_loop(0, chunks, chunk, 0)

    gradients(rows, BLOCK)
    tail = d_copies(rows, BLOCK, chunks)
    far = slice(near, keys)
    gk = (gk_s[:, far] * scale).astype(bf16)
    gv = gv_s[:, far].astype(bf16)
    dw[:, C : 2 * C] += mm(gk, xr[:, far], NT)
    dw[:, 2 * C : 3 * C] += mm(gv, xr[:, far], NT)
    dwo[...] = (dw[...] * grad_scale).astype(bf16)
    halves = range(0, heads, 2)
    p_copies = [
        send(dwo.at[rows_of((partner + k) % heads)], pr.at[i], p_send.at[i], p_recv.at[i], on_mesh(tile, partner))
        for i, k in enumerate(halves)
    ]
    db[...] = (mm(wt[1], gk) + mm(wt[2], gv)).astype(bf16)
    b_copies = []
    for p in range(3):
        there = (tile + groups - offsets[p]) % groups
        for i, to in enumerate(others + [me]):
            b_copies.append(
                send(
                    db.at[rows_of(to), p * border : (p + 1) * border], answers.at[i, p],
                    b_send.at[i, p], b_recv.at[i, p], on_mesh(there, to),
                )
            )
    for copy in tail:
        copy.start()
    for copy in p_copies:
        copy.wait()
    sums = [
        dw[rows_of((me + k) % heads), :] * grad_scale + pr[i].astype(f32) for i, k in enumerate(halves)
    ]
    f_copies = []
    for i, k in enumerate(halves):
        if k:
            fr[i - 1] = sums[i].astype(bf16)
            f_copies.append(
                send(
                    fr.at[i - 1], fr.at[len(halves) - 1 + i - 1], f_send.at[i - 1], f_recv.at[i - 1],
                    on_mesh(tile, (me + k) % heads),
                )
            )
    for copy in f_copies:
        copy.wait()
    total = sums[0]
    for i in range(len(halves) - 1):
        total = total + fr[len(halves) - 1 + i].astype(f32)
    depth = s1.shape[1]
    blocks = 4 * C // 128
    for g in range(groups):
        row, col = (g // blocks) * depth, (g % blocks) * 128
        s1[g] = total[row : row + depth, col : col + 128].astype(bf16)
    r_copies = [
        send(s1.at[to], rs.at[i], r_send.at[i], r_recv.at[i], on_mesh(to, me)) for i, to in enumerate(peers)
    ]

    for copy in b_copies:
        copy.wait()
    for copy in tail:
        copy.wait()

    def d_wait(c, carry):
        for copy in d_copies(c * CHUNK, CHUNK, c):
            copy.wait()
        return carry

    lax.fori_loop(0, chunks, d_wait, 0)
    back = jnp.concatenate(
        [sum(answers[i, p].astype(f32) for i in range(heads)).astype(bf16) for p in range(3)], axis=1
    )
    for h in range(heads):
        for i in range(rows // CHUNK):
            cols = slice(h * rows + i * CHUNK, h * rows + (i + 1) * CHUNK)
            value = dy[:, cols].astype(f32) + bk[h, :, i * CHUNK : (i + 1) * CHUNK].astype(f32)
            value = value + mm(back, chosen[cols, :], NT)
            if i == 0:
                edge = bk[(h - 1) % heads, :, rows:near].astype(f32)
                value = value + jnp.concatenate([edge, jnp.zeros((share, CHUNK - BLOCK), f32)], axis=1)
            result[:, cols] = value
    out_copy = pltpu.make_async_copy(result, d_out, out_sem.at[0])
    out_copy.start()

    for copy in r_copies:
        copy.wait()
    sum_ = s1[tile].astype(f32)
    for i in range(groups - 1):
        sum_ = sum_ + rs[i].astype(f32)
    totals[tile] = sum_.astype(bf16)
    g_copies = [
        send(totals.at[tile], totals.at[tile], g_send.at[i], g_recv.at[i], on_mesh(to, me))
        for i, to in enumerate(peers)
    ]
    for copy in g_copies:
        copy.wait()
    for g in range(groups):
        row, col = (g // blocks) * depth, (g % blocks) * 128
        t, lane = col // C, col % C
        if t < 3:
            gqkv_out[t, row : row + depth, lane : lane + 128] = totals[g].astype(f32)
        else:
            gout_out[row : row + depth, lane : lane + 128] = totals[g].astype(f32)
    out_copy.wait()


def local(tokens, grad_in, w_qkv, w_out, neighbors, send_rows):
    groups = lax.axis_size("tile")
    heads = lax.axis_size("head")
    border = send_rows.shape[2]
    share, full_rows = tokens.shape
    rows = full_rows // heads
    near = rows + BLOCK
    keys = near + 3 * border
    wide = WINDOW + 3 * border
    bf16, f32 = jnp.bfloat16, jnp.float32
    grad_scale = 1.0 / math.sqrt(full_rows * groups)
    vm = pltpu.VMEM
    dma = pltpu.SemaphoreType.DMA
    far = (heads - 1) // 2
    others, peers = heads - 1, groups - 1
    depth = share * 4 * C // 128 // groups
    chunks = rows // CHUNK
    units = HEADS
    any_ = pl.BlockSpec(memory_space=pl.ANY)
    in_vm = pl.BlockSpec(memory_space=vm)
    return pl.pallas_call(
        functools.partial(attention_body, groups, heads, share, border, rows, grad_scale),
        out_shape=(
            jax.ShapeDtypeStruct((share, full_rows), f32),
            jax.ShapeDtypeStruct((3, share, C), f32),
            jax.ShapeDtypeStruct((share, C), f32),
        ),
        in_specs=[any_, any_, any_, any_, in_vm, in_vm],
        out_specs=[any_, in_vm, in_vm],
        scratch_shapes=[
            vm((share, full_rows), bf16),
            vm((share, full_rows), bf16),
            vm((C, keys), bf16),
            vm((C, near), bf16),
            vm((4, C, C), bf16),
            vm((2 * C, C), bf16),
            vm((2 * C, C), bf16),
            vm((3, C, C), bf16),
            vm((full_rows, 3 * border), bf16),
            vm((share, 3 * border), bf16),
            vm((rows // BLOCK * wide, BLOCK), bf16),
            vm((BLOCK, 2 * BLOCK), bf16),
            vm((keys, 2 * C), bf16),
            vm((keys, 2 * C), bf16),
            vm((C, keys), bf16),
            vm((C, keys), bf16),
            vm((units, BLOCK, 2 * BLOCK), bf16),
            vm((units, 2 * C // HEADS, 2 * BLOCK), bf16),
            vm((units, 2 * C // HEADS, 2 * BLOCK), bf16),
            vm((2, wide, 2 * BLOCK), f32),
            vm((2, wide, 2 * BLOCK), bf16),
            vm((2, wide, 2 * BLOCK), bf16),
            vm((C, keys), f32),
            vm((C, keys), f32),
            vm((C, near + BLOCK), f32),
            vm((C, near + BLOCK), f32),
            vm((C, 4 * C), f32),
            vm((C, 4 * C), bf16),
            vm((heads // 2, share, 4 * C), bf16),
            vm((2 * far, share, 4 * C), bf16),
            vm((groups, depth, 128), bf16),
            vm((peers, depth, 128), bf16),
            vm((groups, depth, 128), bf16),
            vm((C, near), bf16),
            vm((heads, share, near), bf16),
            vm((C, 3 * border), bf16),
            vm((heads, 3, share, border), bf16),
            vm((share, full_rows), f32),
        ]
        + [dma((8,))]
        + [dma((2, far + 1))] * 2
        + [dma((far,))] * 2
        + [dma((others,))] * 4
        + [dma((others, chunks))] * 4
        + [dma((3, far + 2))] * 2
        + [dma((far,))] * 2
        + [dma((others, chunks + 1))] * 2
        + [dma((heads, 3))] * 2
        + [dma((heads // 2,))] * 2
        + [dma((far,))] * 2
        + [dma((peers,))] * 4
        + [dma((1,))],
        compiler_params=pltpu.CompilerParams(
            collective_id=0, has_side_effects=True, vmem_limit_bytes=56 * 1024 * 1024
        ),
        name="attend",
    )(tokens, grad_in, w_qkv, w_out, neighbors, send_rows)


def solution(mesh):
    return jax.shard_map(
        local,
        mesh=mesh,
        in_specs=(
            P("head", "tile"),
            P("head", "tile"),
            P(None, "head", None),
            P("head", None),
            P(None, "tile"),
            P("tile", None, None),
        ),
        out_specs=(P("head", "tile"), P(None, "head", None), P("head", None)),
        check_vma=False,
    )
```

```python
import functools
import math

import jax
import jax.numpy as jnp
from jax import lax
from jax.experimental import pallas as pl
from jax.experimental.pallas import tpu as pltpu
from jax.sharding import PartitionSpec as P

C = 256
HEADS = 8
NBR = 9
MARGIN = 64
BLOCK = 2 * MARGIN
WINDOW = 2 * BLOCK
CHUNK = 2 * BLOCK
NEVER = -1.0e30
SLOTS = 3

NN = (((1,), (0,)), ((), ()))
NT = (((1,), (1,)), ((), ()))


def mm(a, b, dims=NN):
    return lax.dot_general(a, b, dims, preferred_element_type=jnp.float32)


def on_mesh(tile, head):
    return {"tile": tile, "head": head}


def greet(peers):
    barrier = pltpu.get_barrier_semaphore()
    for peer in peers:
        pl.semaphore_signal(barrier, inc=1, device_id=peer, device_id_type=pl.DeviceIdType.MESH)
    pl.semaphore_wait(barrier, len(peers))


def remote(src, dst, send_sem, recv_sem, peer):
    return pltpu.make_async_remote_copy(
        src_ref=src,
        dst_ref=dst,
        send_sem=send_sem,
        recv_sem=recv_sem,
        device_id=peer,
        device_id_type=pl.DeviceIdType.MESH,
    )


def send(*args):
    copy = remote(*args)
    copy.start()
    return copy


def attention_body(
    groups, heads, share, border, rows, grad_scale,
    tokens, grad_in, w_qkv, w_out, neighbors_in, send_rows_in,
    d_out, gqkv_out, gout_out,
    tok, dy, xr, yr, wr, wkd, wvp, wt, chosen, mine, bias_s, twice,
    k_s, v_s, kt_s, vt_s, qaug, qdiag, gdiag, e_s, p_s, ds_s,
    gk_s, gv_s, att_s, gq_s, dw, dwo, pr, fr, s1, rs, totals,
    dout, bk, db, answers, result, neighbors, send_rows,
    local_sem, w_send, w_recv, wf_send, wf_recv, xp_send, xp_recv, yp_send, yp_recv,
    x_send, x_recv, y_send, y_recv, e_send, e_recv, ef_send, ef_recv,
    d_send, d_recv, b_send, b_recv, p_send, p_recv, f_send, f_recv,
    r_send, r_recv, g_send, g_recv, out_sem,
):
    head_dim = C // HEADS
    wide_head = 2 * head_dim
    pairs = HEADS // 2
    scale = 1.0 / math.sqrt(head_dim)
    scale2 = scale / math.log(2.0)
    near = rows + BLOCK
    keys = near + 3 * border
    wide = WINDOW + 3 * border
    tiles = wide // BLOCK
    full_rows = rows * heads
    chunks = rows // CHUNK
    bf16, f32 = jnp.bfloat16, jnp.float32
    tile, me = lax.axis_index("tile"), lax.axis_index("head")
    offsets = (1, groups - 1, groups // 2)
    partner = (me // 2) * 2 + 1 - me % 2
    steps = range(2, heads, 2)
    others = [(me + k) % heads for k in range(1, heads)]
    peers = [(tile + k) % groups for k in range(1, groups)]

    def rows_of(index):
        return pl.ds(pl.multiple_of(index * share, share), share)

    def lanes(start, size):
        return pl.ds(pl.multiple_of(start, BLOCK), size)

    greet(
        [on_mesh(tile, to) for to in others]
        + [on_mesh(to, me) for to in peers]
        + [on_mesh((tile + offset) % groups, to) for offset in offsets for to in others]
    )

    locals_ = [pltpu.make_async_copy(tokens, tok, local_sem.at[0])]
    pairs_of = ((tokens, xr), (grad_in, yr))
    own = lanes(me * rows, rows)
    after = lanes(((me + 1) % heads) * rows, BLOCK)
    for i, (src, dst) in enumerate(pairs_of):
        locals_.append(pltpu.make_async_copy(src.at[:, own], dst.at[rows_of(me), 0:rows], local_sem.at[1 + 2 * i]))
        locals_.append(
            pltpu.make_async_copy(src.at[:, after], dst.at[rows_of(me), rows:near], local_sem.at[2 + 2 * i])
        )
    locals_.append(pltpu.make_async_copy(w_qkv, wr.at[0:3, rows_of(me), :], local_sem.at[5]))
    locals_.append(pltpu.make_async_copy(w_out, wr.at[3, rows_of(me), :], local_sem.at[6]))
    locals_.append(pltpu.make_async_copy(grad_in, dy, local_sem.at[7]))
    locals_.append(pltpu.make_async_copy(neighbors_in, neighbors, local_sem.at[8]))
    rows_copy = pltpu.make_async_copy(send_rows_in, send_rows, local_sem.at[9])
    rows_copy.start()
    for copy in locals_:
        copy.start()

    w_copies = []
    for i, to in enumerate([(me + k) % heads for k in steps] + [partner]):
        w_copies.append(
            [
                send(w_qkv, wr.at[0:3, rows_of(me), :], w_send.at[0, i], w_recv.at[0, i], on_mesh(tile, to)),
                send(w_out, wr.at[3, rows_of(me), :], w_send.at[1, i], w_recv.at[1, i], on_mesh(tile, to)),
            ]
        )
    def piece(c):
        return lanes(BLOCK + c * CHUNK, CHUNK)

    def start_chunk(c):
        first = BLOCK + c * CHUNK
        for i, to in enumerate(others):
            for src, dst, ss, rr in ((tokens, xr, x_send, x_recv), (grad_in, yr, y_send, y_recv)):
                for at in (first, first + BLOCK):
                    frm = (to * rows + at) % full_rows
                    send(
                        src.at[:, lanes(frm, BLOCK)], dst.at[rows_of(me), lanes(at, BLOCK)],
                        ss.at[i, c], rr.at[i, c], on_mesh(tile, to),
                    )

    def chunk_copies(c):
        copies = []
        for i, to in enumerate(others):
            for src, dst, ss, rr in ((tokens, xr, x_send, x_recv), (grad_in, yr, y_send, y_recv)):
                copies.append(
                    remote(
                        src.at[:, 0:CHUNK], dst.at[rows_of(me), piece(c)],
                        ss.at[i, c], rr.at[i, c], on_mesh(tile, to),
                    )
                )
        return copies

    rows_copy.wait()
    flat = jnp.concatenate([send_rows[0, p : p + 1, :] for p in range(3)], axis=1)

    def choose(i, carry):
        ids = lax.broadcasted_iota(jnp.int32, (CHUNK, 3 * border), 0) + i * CHUNK
        at = pl.ds(pl.multiple_of(i * CHUNK, CHUNK), CHUNK)
        chosen[at, :] = jnp.where(ids == flat, 1.0, 0.0).astype(bf16)
        return carry

    lax.fori_loop(0, full_rows // CHUNK, choose, 0)
    locals_[0].wait()
    mine[...] = mm(tok[...], chosen[...]).astype(bf16)
    e_copies = []
    for p in range(3):
        there = (tile + offsets[p]) % groups
        cols = slice(near + p * border, near + (p + 1) * border)
        for i, to in enumerate([(me + k) % heads for k in steps] + [me, partner]):
            e_copies.append(
                send(
                    mine.at[:, p * border : (p + 1) * border], xr.at[rows_of(me), cols],
                    e_send.at[p, i], e_recv.at[p, i], on_mesh(there, to),
                )
            )

    moving = []
    for i, to in enumerate(others):
        for src, dst, ss, rr in ((tokens, xr, xp_send, xp_recv), (grad_in, yr, yp_send, yp_recv)):
            moving.append(
                send(src.at[:, lanes(to * rows, BLOCK)], dst.at[rows_of(me), 0:BLOCK], ss.at[i], rr.at[i], on_mesh(tile, to))
            )

    start_chunk(0)

    locals_[8].wait()
    def mask(b, carry):
        start = pl.multiple_of(b * BLOCK, BLOCK)
        here = me * rows + start
        one = neighbors[:, lanes(here, BLOCK)]
        two = neighbors[:, lanes((here + BLOCK) % full_rows, BLOCK)]
        ring = jnp.concatenate([one[:, MARGIN:], two[:, :MARGIN]], axis=1)
        along = ring - me * rows
        along = jnp.where(along < 0, along + full_rows, along)
        picks = jnp.where(ring < full_rows, along - start, ring - full_rows + WINDOW)
        for t in range(tiles):
            ids = lax.broadcasted_iota(jnp.int32, (BLOCK, BLOCK), 0) + t * BLOCK
            count = jnp.zeros((BLOCK, BLOCK), f32)
            for j in range(NBR):
                count = count + jnp.where(ids == picks[j : j + 1, :], 1.0, 0.0)
            bias = jnp.where(count > 0.0, jnp.log2(jnp.maximum(count, 1.0)), NEVER)
            bias_s[pl.ds(pl.multiple_of(b * wide + t * BLOCK, BLOCK), BLOCK), :] = bias.astype(bf16)
        return carry

    lax.fori_loop(0, rows // BLOCK, mask, 0)
    qaug[...] = jnp.zeros_like(qaug)
    qdiag[...] = jnp.zeros_like(qdiag)
    gdiag[...] = jnp.zeros_like(gdiag)
    gk_s[...] = jnp.zeros_like(gk_s)
    gv_s[...] = jnp.zeros_like(gv_s)
    dw[...] = jnp.zeros_like(dw)
    att_s[...] = jnp.zeros_like(att_s)
    gq_s[...] = jnp.zeros_like(gq_s)
    diag = jnp.where(
        lax.broadcasted_iota(jnp.int32, (BLOCK, BLOCK), 0) == lax.broadcasted_iota(jnp.int32, (BLOCK, BLOCK), 1), 1.0, 0.0
    ).astype(bf16)
    twice[:, :BLOCK] = diag
    twice[:, BLOCK:] = diag
    wvp[...] = jnp.zeros_like(wvp)

    last = []
    for i, k in enumerate(steps):
        for copy in w_copies[i]:
            copy.wait()
        block_ref = wr.at[:, rows_of((me + heads - k) % heads), :]
        last.append(send(block_ref, block_ref, wf_send.at[i], wf_recv.at[i], on_mesh(tile, partner)))
    for copy in w_copies[len(steps)]:
        copy.wait()
    for copy in e_copies:
        copy.wait()
    for i, k in enumerate(steps):
        block_ref = xr.at[rows_of((me + heads - k) % heads), near:keys]
        last.append(send(block_ref, block_ref, ef_send.at[i], ef_recv.at[i], on_mesh(tile, partner)))
    for copy in locals_[1:8]:
        copy.wait()
    for i in range(len(steps)):
        last[i].wait()
    for t in range(3):
        wt[t] = wr[t].T
    for pair in range(pairs):
        chan = slice(pair * wide_head, (pair + 1) * wide_head)
        base = pair * 2 * wide_head
        wkd[base : base + wide_head, :] = wr[1, chan, :]
        wkd[base + wide_head : base + 2 * wide_head, :] = wr[1, chan, :]
        wvp[base : base + wide_head, :] = wr[2, chan, :]

    lane_id = lax.broadcasted_iota(jnp.int32, (1, 2 * C), 1) % (2 * wide_head)
    ones = jnp.where((lane_id >= wide_head) & (lane_id < wide_head + 3), 1.0, 0.0)

    def project(at_rows, at_cols):
        x = xr[:, at_cols]
        xt = x.T
        k_s[at_rows, :] = mm(xt, wkd[...], NT).astype(bf16)
        v_s[at_rows, :] = (mm(xt, wvp[...], NT) + ones).astype(bf16)
        kt_s[:, at_cols] = mm(wr[1], x).astype(bf16)
        vt_s[:, at_cols] = mm(wr[2], x).astype(bf16)

    for copy in moving:
        copy.wait()
    project(slice(0, BLOCK), slice(0, BLOCK))
    for i in range(len(steps)):
        last[len(steps) + i].wait()
    project(slice(near, keys), slice(near, keys))

    def gradients(cols, size):
        around = lanes(cols, size + BLOCK)
        gq = pltpu.roll(gq_s[:, around], size + MARGIN, 1)[:, :size].astype(bf16)
        att = pltpu.roll(att_s[:, around], size + MARGIN, 1)[:, :size].astype(bf16)
        here = lanes(cols, size)
        gk = (gk_s[:, here] * scale).astype(bf16)
        gv = gv_s[:, here].astype(bf16)
        x = xr[:, here]
        for t, (left, right) in enumerate(((gq, x), (att, yr[:, here]), (gk, x), (gv, x))):
            dw[:, t * C : (t + 1) * C] += mm(left, right, NT)
        d = mm(wt[0], gq) + mm(wt[1], gk) + mm(wt[2], gv)
        dout[:, here] = d.astype(bf16)
        bk[me, :, here] = dout[rows_of(me), here]

    def d_copies(cols, size, c):
        return [
            remote(
                dout.at[rows_of(to), lanes(cols, size)], bk.at[me, :, lanes(cols, size)],
                d_send.at[i, c], d_recv.at[i, c], on_mesh(tile, to),
            )
            for i, to in enumerate(others)
        ]

    def chunk(c, carry):
        base = pl.multiple_of(c * CHUNK, CHUNK)
        for copy in chunk_copies(c):
            copy.wait()

        @pl.when(c + 1 < chunks)
        def _():
            start_chunk(c + 1)

        @pl.when(c + 1 == chunks)
        def _():
            for before in range(chunks - 2):
                for copy in d_copies(before * CHUNK, CHUNK, before):
                    copy.start()

        project(pl.ds(pl.multiple_of(base + BLOCK, BLOCK), CHUNK), piece(c))
        gradients(jnp.maximum(c - 1, 0) * CHUNK, CHUNK)
        around = lanes(base, CHUNK + BLOCK)
        q = pltpu.roll(mm(wr[0], xr[:, around]), CHUNK + MARGIN, 1)[:, :CHUNK].astype(bf16)
        g = pltpu.roll(mm(wr[3], yr[:, around]), CHUNK + MARGIN, 1)[:, :CHUNK].astype(bf16)
        scaled = q.astype(f32) * scale2
        high = scaled.astype(bf16)
        low = (scaled - high.astype(f32)).astype(bf16)
        for half in range(2):
            cols = slice(half * BLOCK, (half + 1) * BLOCK)
            for pair in range(pairs):
                u = half * pairs + pair
                for side in range(2):
                    chan = slice((pair * 2 + side) * head_dim, (pair * 2 + side + 1) * head_dim)
                    at = slice(side * head_dim, (side + 1) * head_dim)
                    under = slice(wide_head + side * head_dim, wide_head + (side + 1) * head_dim)
                    lane = slice(side * BLOCK, (side + 1) * BLOCK)
                    qaug[u, at, lane] = high[chan, cols]
                    qaug[u, under, lane] = low[chan, cols]
                    qdiag[u, at, lane] = q[chan, cols]
                    gdiag[u, at, lane] = g[chan, cols]

        units = 2 * pairs
        total, inv, right = {}, {}, {}

        def place(u):
            half, pair = u // pairs, u % pairs
            start = pl.multiple_of(base + half * BLOCK, BLOCK)
            return start, pair, slice(pair * wide_head, (pair + 1) * wide_head)

        def part_rows(part):
            return (slice(0, WINDOW), 0) if part == 0 else (slice(WINDOW, wide), WINDOW)

        def key_rows(u, part):
            return pl.ds(place(u)[0], WINDOW) if part == 0 else slice(near, keys)

        def score(u, part):
            pair = u % pairs
            at, row = part_rows(part)
            left = jnp.concatenate(
                [
                    k_s[key_rows(u, part), pair * BLOCK : (pair + 1) * BLOCK],
                    bias_s[pl.ds(pl.multiple_of((c * 2 + u // pairs) * wide + row, BLOCK), at.stop - row), :],
                ],
                axis=1,
            )
            e = jnp.exp2(mm(left, jnp.concatenate([qaug[u], twice[...]], axis=0)))
            some = jnp.sum(e.reshape((at.stop - row) // 8, 8, 2 * BLOCK), axis=0)
            total[u] = some if part == 0 else total[u] + some
            e_s[u % SLOTS, at, :] = e

        def normal(u, part):
            if part == 0:
                inv[u] = 1.0 / jnp.sum(total[u], axis=0, keepdims=True)
            at, _ = part_rows(part)
            p = e_s[u % SLOTS, at, :] * inv[u]
            e_s[u % SLOTS, at, :] = p
            p_s[u % 2, at, :] = p.astype(bf16)

        def spans(u):
            return (lanes(place(u)[0], WINDOW), slice(0, WINDOW)), (slice(near, keys), slice(WINDOW, wide))

        def attend(u):
            start, pair, chan = place(u)
            att = jnp.zeros((wide_head, 2 * BLOCK), f32)
            for span, at in spans(u):
                att = att + mm(vt_s[chan, span], p_s[u % 2, at, :])
            gd = gdiag[u]
            mean = -jnp.sum(att * gd.astype(f32), axis=0, keepdims=True)
            m0 = mean.astype(bf16).astype(f32)
            m1 = (mean - m0).astype(bf16).astype(f32)
            m2 = mean - m0 - m1
            ids = lax.broadcasted_iota(jnp.int32, (16, 2 * BLOCK), 0)
            rows3 = jnp.where(ids == 0, m0, jnp.where(ids == 1, m1, jnp.where(ids == 2, m2, 0.0))).astype(bf16)
            right[u] = jnp.concatenate([gd, rows3, jnp.zeros((wide_head - 16, 2 * BLOCK), bf16)], axis=0)
            cols = lanes(start + BLOCK, BLOCK)
            first = pair * wide_head
            att_s[first : first + head_dim, cols] = att[:head_dim, :BLOCK]
            att_s[first + head_dim : first + wide_head, cols] = att[head_dim:, BLOCK:]

        def value_grad(u):
            _, _, chan = place(u)
            for span, at in spans(u):
                gv_s[chan, span] += mm(gdiag[u], p_s[u % 2, at, :], NT)

        def dscore(u, part):
            pair = u % pairs
            at, _ = part_rows(part)
            dp = mm(v_s[key_rows(u, part), pair * BLOCK : (pair + 1) * BLOCK], right[u])
            ds_s[u % 2, at, :] = (e_s[u % SLOTS, at, :] * dp).astype(bf16)

        def query_grad(u):
            start, pair, chan = place(u)
            gq = jnp.zeros((wide_head, 2 * BLOCK), f32)
            for span, at in spans(u):
                gq = gq + mm(kt_s[chan, span], ds_s[u % 2, at, :])
            gq = gq * scale
            cols = lanes(start + BLOCK, BLOCK)
            first = pair * wide_head
            gq_s[first : first + head_dim, cols] = gq[:head_dim, :BLOCK]
            gq_s[first + head_dim : first + wide_head, cols] = gq[head_dim:, BLOCK:]

        def key_grad(u):
            _, _, chan = place(u)
            for span, at in spans(u):
                gk_s[chan, span] += mm(qdiag[u], ds_s[u % 2, at, :], NT)

        for i in range(units + 2):
            for part in range(2):
                if i < units:
                    score(i, part)
                if i >= 2:
                    dscore(i - 2, part)
                if 1 <= i <= units:
                    normal(i - 1, part)
            if 1 <= i <= units:
                attend(i - 1)
            if i >= 2:
                query_grad(i - 2)
            if 1 <= i <= units:
                value_grad(i - 1)
            if i >= 2:
                key_grad(i - 2)

        return carry

    lax.fori_loop(0, chunks, chunk, 0)

    gradients(rows - CHUNK, CHUNK + BLOCK)
    tail = d_copies((chunks - 2) * CHUNK, CHUNK, chunks - 2) + d_copies((chunks - 1) * CHUNK, CHUNK, chunks - 1) + d_copies(rows, BLOCK, chunks)
    far = slice(near, keys)
    halves = range(0, heads, 2)
    half_cols = 2 * C

    def to_partner(part):
        cols = slice(part * half_cols, (part + 1) * half_cols)
        dwo[part] = (dw[:, cols] * grad_scale).astype(bf16)
        return [
            send(
                dwo.at[part, rows_of((partner + k) % heads)], pr.at[part, i],
                p_send.at[part, i], p_recv.at[part, i], on_mesh(tile, partner),
            )
            for i, k in enumerate(halves)
        ]

    kept, f_copies, r_copies, g_copies = {}, {}, {}, {}

    def to_far(part, copies):
        cols = slice(part * half_cols, (part + 1) * half_cols)
        for copy in copies:
            copy.wait()
        f_copies[part] = []
        for i, k in enumerate(halves):
            value = dw[rows_of((me + k) % heads), cols] * grad_scale + pr[part, i].astype(f32)
            if k:
                fr[part, i - 1] = value.astype(bf16)
                f_copies[part].append(
                    send(
                        fr.at[part, i - 1], fr.at[part, len(halves) - 1 + i - 1],
                        f_send.at[part, i - 1], f_recv.at[part, i - 1], on_mesh(tile, (me + k) % heads),
                    )
                )
            else:
                kept[part] = value

    depth = s1.shape[2]
    blocks = half_cols // 128

    def to_tiles(part):
        for copy in f_copies[part]:
            copy.wait()
        total = kept[part]
        for i in range(len(halves) - 1):
            total = total + fr[part, len(halves) - 1 + i].astype(f32)
        for g in range(groups):
            row, col = (g // blocks) * depth, (g % blocks) * 128
            s1[part, g] = total[row : row + depth, col : col + 128].astype(bf16)
        r_copies[part] = [
            send(s1.at[part, to], rs.at[part, i], r_send.at[part, i], r_recv.at[part, i], on_mesh(to, me))
            for i, to in enumerate(peers)
        ]

    def from_tiles(part):
        for copy in r_copies[part]:
            copy.wait()
        total = s1[part, tile].astype(f32)
        for i in range(groups - 1):
            total = total + rs[part, i].astype(f32)
        totals[part, tile] = total.astype(bf16)
        g_copies[part] = [
            send(
                totals.at[part, tile], totals.at[part, tile],
                g_send.at[part, i], g_recv.at[part, i], on_mesh(to, me),
            )
            for i, to in enumerate(peers)
        ]

    first = to_partner(0)
    gk = (gk_s[:, far] * scale).astype(bf16)
    gv = gv_s[:, far].astype(bf16)
    dw[:, 2 * C : 3 * C] += mm(gk, xr[:, far], NT)
    dw[:, 3 * C : 4 * C] += mm(gv, xr[:, far], NT)
    second = to_partner(1)
    to_far(0, first)
    to_far(1, second)
    db[...] = (mm(wt[1], gk) + mm(wt[2], gv)).astype(bf16)
    b_copies = []
    for p in range(3):
        there = (tile + groups - offsets[p]) % groups
        for i, to in enumerate(others + [me]):
            b_copies.append(
                send(
                    db.at[rows_of(to), p * border : (p + 1) * border], answers.at[i, p],
                    b_send.at[i, p], b_recv.at[i, p], on_mesh(there, to),
                )
            )
    for copy in tail:
        copy.start()
    to_tiles(0)
    to_tiles(1)
    from_tiles(0)
    from_tiles(1)

    for copy in b_copies:
        copy.wait()
    for copy in tail:
        copy.wait()

    def d_wait(c, carry):
        for copy in d_copies(c * CHUNK, CHUNK, c):
            copy.wait()
        return carry

    lax.fori_loop(0, chunks - 2, d_wait, 0)
    back = jnp.concatenate(
        [sum(answers[i, p].astype(f32) for i in range(heads)).astype(bf16) for p in range(3)], axis=1
    )
    for h in range(heads):
        for i in range(rows // CHUNK):
            cols = slice(h * rows + i * CHUNK, h * rows + (i + 1) * CHUNK)
            value = dy[:, cols].astype(f32) + bk[h, :, i * CHUNK : (i + 1) * CHUNK].astype(f32)
            value = value + mm(back, chosen[cols, :], NT)
            if i == 0:
                edge = bk[(h - 1) % heads, :, rows:near].astype(f32)
                value = value + jnp.concatenate([edge, jnp.zeros((share, CHUNK - BLOCK), f32)], axis=1)
            result[:, cols] = value
    out_copy = pltpu.make_async_copy(result, d_out, out_sem.at[0])
    out_copy.start()

    for part in range(2):
        for copy in g_copies[part]:
            copy.wait()
        for g in range(groups):
            row, col = (g // blocks) * depth, (g % blocks) * 128
            lane = col % C
            value = totals[part, g].astype(f32)
            if part == 0 and col >= C:
                gout_out[row : row + depth, lane : lane + 128] = value
            else:
                gqkv_out[part + col // C, row : row + depth, lane : lane + 128] = value
    out_copy.wait()


def local(tokens, grad_in, w_qkv, w_out, neighbors, send_rows):
    groups = lax.axis_size("tile")
    heads = lax.axis_size("head")
    border = send_rows.shape[2]
    share, full_rows = tokens.shape
    rows = full_rows // heads
    near = rows + BLOCK
    keys = near + 3 * border
    wide = WINDOW + 3 * border
    bf16, f32 = jnp.bfloat16, jnp.float32
    grad_scale = 1.0 / math.sqrt(full_rows * groups)
    vm = pltpu.VMEM
    dma = pltpu.SemaphoreType.DMA
    far = (heads - 1) // 2
    others, peers = heads - 1, groups - 1
    depth = share * 2 * C // 128 // groups
    chunks = rows // CHUNK
    units = HEADS
    any_ = pl.BlockSpec(memory_space=pl.ANY)
    in_vm = pl.BlockSpec(memory_space=vm)
    return pl.pallas_call(
        functools.partial(attention_body, groups, heads, share, border, rows, grad_scale),
        out_shape=(
            jax.ShapeDtypeStruct((share, full_rows), f32),
            jax.ShapeDtypeStruct((3, share, C), f32),
            jax.ShapeDtypeStruct((share, C), f32),
        ),
        in_specs=[any_] * 6,
        out_specs=[any_, in_vm, in_vm],
        scratch_shapes=[
            vm((share, full_rows), bf16),
            vm((share, full_rows), bf16),
            vm((C, keys), bf16),
            vm((C, near), bf16),
            vm((4, C, C), bf16),
            vm((2 * C, C), bf16),
            vm((2 * C, C), bf16),
            vm((3, C, C), bf16),
            vm((full_rows, 3 * border), bf16),
            vm((share, 3 * border), bf16),
            vm((rows // BLOCK * wide, BLOCK), bf16),
            vm((BLOCK, 2 * BLOCK), bf16),
            vm((keys, 2 * C), bf16),
            vm((keys, 2 * C), bf16),
            vm((C, keys), bf16),
            vm((C, keys), bf16),
            vm((units, BLOCK, 2 * BLOCK), bf16),
            vm((units, 2 * C // HEADS, 2 * BLOCK), bf16),
            vm((units, 2 * C // HEADS, 2 * BLOCK), bf16),
            vm((SLOTS, wide, 2 * BLOCK), f32),
            vm((2, wide, 2 * BLOCK), bf16),
            vm((2, wide, 2 * BLOCK), bf16),
            vm((C, keys), f32),
            vm((C, keys), f32),
            vm((C, near + BLOCK), f32),
            vm((C, near + BLOCK), f32),
            vm((C, 4 * C), f32),
            vm((2, C, 2 * C), bf16),
            vm((2, heads // 2, share, 2 * C), bf16),
            vm((2, 2 * far, share, 2 * C), bf16),
            vm((2, groups, depth, 128), bf16),
            vm((2, peers, depth, 128), bf16),
            vm((2, groups, depth, 128), bf16),
            vm((C, near), bf16),
            vm((heads, share, near), bf16),
            vm((C, 3 * border), bf16),
            vm((heads, 3, share, border), bf16),
            vm((share, full_rows), f32),
            vm((NBR, full_rows), jnp.int32),
            vm((1, 3, border), jnp.int32),
        ]
        + [dma((10,))]
        + [dma((2, far + 1))] * 2
        + [dma((far,))] * 2
        + [dma((others,))] * 4
        + [dma((others, chunks))] * 4
        + [dma((3, far + 2))] * 2
        + [dma((far,))] * 2
        + [dma((others, chunks + 1))] * 2
        + [dma((heads, 3))] * 2
        + [dma((2, heads // 2))] * 2
        + [dma((2, far))] * 2
        + [dma((2, peers))] * 4
        + [dma((1,))],
        compiler_params=pltpu.CompilerParams(
            collective_id=0, has_side_effects=True, vmem_limit_bytes=56 * 1024 * 1024
        ),
        name="attend",
    )(tokens, grad_in, w_qkv, w_out, neighbors, send_rows)


def solution(mesh):
    return jax.shard_map(
        local,
        mesh=mesh,
        in_specs=(
            P("head", "tile"),
            P("head", "tile"),
            P(None, "head", None),
            P("head", None),
            P(None, "tile"),
            P("tile", None, None),
        ),
        out_specs=(P("head", "tile"), P(None, "head", None), P("head", None)),
        check_vma=False,
    )
```

```python
import functools
import math

import jax
import jax.numpy as jnp
from jax import lax
from jax.experimental import pallas as pl
from jax.experimental.pallas import tpu as pltpu
from jax.sharding import PartitionSpec as P

C = 256
HEADS = 8
NBR = 9
MARGIN = 64
BLOCK = 2 * MARGIN
WINDOW = 2 * BLOCK
CHUNK = 2 * BLOCK
NEVER = -1.0e30
SLOTS = 4

NN = (((1,), (0,)), ((), ()))
NT = (((1,), (1,)), ((), ()))


def mm(a, b, dims=NN):
    return lax.dot_general(a, b, dims, preferred_element_type=jnp.float32)


def on_mesh(tile, head):
    return {"tile": tile, "head": head}


def greet(peers):
    barrier = pltpu.get_barrier_semaphore()
    for peer in peers:
        pl.semaphore_signal(barrier, inc=1, device_id=peer, device_id_type=pl.DeviceIdType.MESH)
    pl.semaphore_wait(barrier, len(peers))


def remote(src, dst, send_sem, recv_sem, peer):
    return pltpu.make_async_remote_copy(
        src_ref=src,
        dst_ref=dst,
        send_sem=send_sem,
        recv_sem=recv_sem,
        device_id=peer,
        device_id_type=pl.DeviceIdType.MESH,
    )


def send(*args):
    copy = remote(*args)
    copy.start()
    return copy


def attention_body(
    groups, heads, share, border, rows, grad_scale,
    tokens, grad_in, w_qkv, w_out, neighbors_in, send_rows_in,
    d_out, gqkv_out, gout_out,
    tok, dy, xr, yr, wr, wkd, wvp, wt, chosen, mine, bias_s, twice,
    k_s, v_s, kt_s, vt_s, qaug, qdiag, gdiag, e_s, p_s, ds_s,
    gk_s, gv_s, att_s, gq_s, dw, dwo, pr, fr, s1, rs, totals,
    dout, bk, db, answers, result, br, neighbors, send_rows,
    local_sem, w_send, w_recv, wf_send, wf_recv, xp_send, xp_recv, yp_send, yp_recv,
    x_send, x_recv, y_send, y_recv, e_send, e_recv, ef_send, ef_recv,
    d_send, d_recv, b_send, b_recv, a_send, a_recv, p_send, p_recv, f_send, f_recv,
    r_send, r_recv, g_send, g_recv, out_sem,
):
    head_dim = C // HEADS
    wide_head = 2 * head_dim
    pairs = HEADS // 2
    scale = 1.0 / math.sqrt(head_dim)
    scale2 = scale / math.log(2.0)
    near = rows + BLOCK
    keys = near + 3 * border
    wide = WINDOW + 3 * border
    tiles = wide // BLOCK
    full_rows = rows * heads
    chunks = rows // CHUNK
    bf16, f32 = jnp.bfloat16, jnp.float32
    tile, me = lax.axis_index("tile"), lax.axis_index("head")
    offsets = (1, groups - 1, groups // 2)
    partner = (me // 2) * 2 + 1 - me % 2
    steps = range(2, heads, 2)
    others = [(me + k) % heads for k in range(1, heads)]
    peers = [(tile + k) % groups for k in range(1, groups)]

    def rows_of(index):
        return pl.ds(pl.multiple_of(index * share, share), share)

    def lanes(start, size):
        return pl.ds(pl.multiple_of(start, BLOCK), size)

    greet(
        [on_mesh(tile, to) for to in others]
        + [on_mesh(to, me) for to in peers]
        + [on_mesh((tile + offset) % groups, to) for offset in offsets for to in others]
    )

    locals_ = [pltpu.make_async_copy(tokens, tok, local_sem.at[0])]
    pairs_of = ((tokens, xr), (grad_in, yr))
    own = lanes(me * rows, rows)
    after = lanes(((me + 1) % heads) * rows, BLOCK)
    for i, (src, dst) in enumerate(pairs_of):
        locals_.append(pltpu.make_async_copy(src.at[:, own], dst.at[rows_of(me), 0:rows], local_sem.at[1 + 2 * i]))
        locals_.append(
            pltpu.make_async_copy(src.at[:, after], dst.at[rows_of(me), rows:near], local_sem.at[2 + 2 * i])
        )
    locals_.append(pltpu.make_async_copy(w_qkv, wr.at[0:3, rows_of(me), :], local_sem.at[5]))
    locals_.append(pltpu.make_async_copy(w_out, wr.at[3, rows_of(me), :], local_sem.at[6]))
    locals_.append(pltpu.make_async_copy(grad_in, dy, local_sem.at[7]))
    locals_.append(pltpu.make_async_copy(neighbors_in, neighbors, local_sem.at[8]))
    rows_copy = pltpu.make_async_copy(send_rows_in, send_rows, local_sem.at[9])
    rows_copy.start()
    for copy in locals_:
        copy.start()

    w_copies = []
    for i, to in enumerate([(me + k) % heads for k in steps] + [partner]):
        w_copies.append(
            [
                send(w_qkv, wr.at[0:3, rows_of(me), :], w_send.at[0, i], w_recv.at[0, i], on_mesh(tile, to)),
                send(w_out, wr.at[3, rows_of(me), :], w_send.at[1, i], w_recv.at[1, i], on_mesh(tile, to)),
            ]
        )
    def piece(c):
        return lanes(BLOCK + c * CHUNK, CHUNK)

    def start_chunk(c):
        first = BLOCK + c * CHUNK
        for i, to in enumerate(others):
            for src, dst, ss, rr in ((tokens, xr, x_send, x_recv), (grad_in, yr, y_send, y_recv)):
                for at in (first, first + BLOCK):
                    frm = (to * rows + at) % full_rows
                    send(
                        src.at[:, lanes(frm, BLOCK)], dst.at[rows_of(me), lanes(at, BLOCK)],
                        ss.at[i, c], rr.at[i, c], on_mesh(tile, to),
                    )

    def chunk_copies(c):
        copies = []
        for i, to in enumerate(others):
            for src, dst, ss, rr in ((tokens, xr, x_send, x_recv), (grad_in, yr, y_send, y_recv)):
                copies.append(
                    remote(
                        src.at[:, 0:CHUNK], dst.at[rows_of(me), piece(c)],
                        ss.at[i, c], rr.at[i, c], on_mesh(tile, to),
                    )
                )
        return copies

    rows_copy.wait()
    flat = jnp.concatenate([send_rows[0, p : p + 1, :] for p in range(3)], axis=1)

    def choose(i, carry):
        ids = lax.broadcasted_iota(jnp.int32, (CHUNK, 3 * border), 0) + i * CHUNK
        at = pl.ds(pl.multiple_of(i * CHUNK, CHUNK), CHUNK)
        chosen[at, :] = jnp.where(ids == flat, 1.0, 0.0).astype(bf16)
        return carry

    lax.fori_loop(0, full_rows // CHUNK, choose, 0)
    locals_[0].wait()
    mine[...] = mm(tok[...], chosen[...]).astype(bf16)
    e_copies = []
    for p in range(3):
        there = (tile + offsets[p]) % groups
        cols = slice(near + p * border, near + (p + 1) * border)
        for i, to in enumerate([(me + k) % heads for k in steps] + [me, partner]):
            e_copies.append(
                send(
                    mine.at[:, p * border : (p + 1) * border], xr.at[rows_of(me), cols],
                    e_send.at[p, i], e_recv.at[p, i], on_mesh(there, to),
                )
            )

    moving = []
    for i, to in enumerate(others):
        for src, dst, ss, rr in ((tokens, xr, xp_send, xp_recv), (grad_in, yr, yp_send, yp_recv)):
            moving.append(
                send(src.at[:, lanes(to * rows, BLOCK)], dst.at[rows_of(me), 0:BLOCK], ss.at[i], rr.at[i], on_mesh(tile, to))
            )

    start_chunk(0)

    locals_[8].wait()
    def mask(b, carry):
        start = pl.multiple_of(b * BLOCK, BLOCK)
        here = me * rows + start
        one = neighbors[:, lanes(here, BLOCK)]
        two = neighbors[:, lanes((here + BLOCK) % full_rows, BLOCK)]
        ring = jnp.concatenate([one[:, MARGIN:], two[:, :MARGIN]], axis=1)
        along = ring - me * rows
        along = jnp.where(along < 0, along + full_rows, along)
        picks = jnp.where(ring < full_rows, along - start, ring - full_rows + WINDOW)
        for t in range(tiles):
            ids = lax.broadcasted_iota(jnp.int32, (BLOCK, BLOCK), 0) + t * BLOCK
            count = jnp.zeros((BLOCK, BLOCK), f32)
            for j in range(NBR):
                count = count + jnp.where(ids == picks[j : j + 1, :], 1.0, 0.0)
            bias = jnp.where(count > 0.0, jnp.log2(jnp.maximum(count, 1.0)), NEVER)
            bias_s[pl.ds(pl.multiple_of(b * wide + t * BLOCK, BLOCK), BLOCK), :] = bias.astype(bf16)
        return carry

    lax.fori_loop(0, rows // BLOCK, mask, 0)
    qaug[...] = jnp.zeros_like(qaug)
    qdiag[...] = jnp.zeros_like(qdiag)
    gdiag[...] = jnp.zeros_like(gdiag)
    gk_s[...] = jnp.zeros_like(gk_s)
    gv_s[...] = jnp.zeros_like(gv_s)
    dw[...] = jnp.zeros_like(dw)
    att_s[...] = jnp.zeros_like(att_s)
    gq_s[...] = jnp.zeros_like(gq_s)
    diag = jnp.where(
        lax.broadcasted_iota(jnp.int32, (BLOCK, BLOCK), 0) == lax.broadcasted_iota(jnp.int32, (BLOCK, BLOCK), 1), 1.0, 0.0
    ).astype(bf16)
    twice[:, :BLOCK] = diag
    twice[:, BLOCK:] = diag
    wvp[...] = jnp.zeros_like(wvp)

    last = []
    for i, k in enumerate(steps):
        for copy in w_copies[i]:
            copy.wait()
        block_ref = wr.at[:, rows_of((me + heads - k) % heads), :]
        last.append(send(block_ref, block_ref, wf_send.at[i], wf_recv.at[i], on_mesh(tile, partner)))
    for copy in w_copies[len(steps)]:
        copy.wait()
    for copy in e_copies:
        copy.wait()
    for i, k in enumerate(steps):
        block_ref = xr.at[rows_of((me + heads - k) % heads), near:keys]
        last.append(send(block_ref, block_ref, ef_send.at[i], ef_recv.at[i], on_mesh(tile, partner)))
    for copy in locals_[1:8]:
        copy.wait()
    for i in range(len(steps)):
        last[i].wait()
    for t in range(3):
        wt[t] = wr[t].T
    for pair in range(pairs):
        chan = slice(pair * wide_head, (pair + 1) * wide_head)
        base = pair * 2 * wide_head
        wkd[base : base + wide_head, :] = wr[1, chan, :]
        wkd[base + wide_head : base + 2 * wide_head, :] = wr[1, chan, :]
        wvp[base : base + wide_head, :] = wr[2, chan, :]

    lane_id = lax.broadcasted_iota(jnp.int32, (1, 2 * C), 1) % (2 * wide_head)
    ones = jnp.where((lane_id >= wide_head) & (lane_id < wide_head + 3), 1.0, 0.0)

    def project(at_rows, at_cols):
        x = xr[:, at_cols]
        xt = x.T
        k_s[at_rows, :] = mm(xt, wkd[...], NT).astype(bf16)
        v_s[at_rows, :] = (mm(xt, wvp[...], NT) + ones).astype(bf16)
        kt_s[:, at_cols] = mm(wr[1], x).astype(bf16)
        vt_s[:, at_cols] = mm(wr[2], x).astype(bf16)

    for copy in moving:
        copy.wait()
    project(slice(0, BLOCK), slice(0, BLOCK))
    for i in range(len(steps)):
        last[len(steps) + i].wait()
    project(slice(near, keys), slice(near, keys))

    def shifted(ref, cols, size):
        return pltpu.roll(ref[:, lanes(cols, size + BLOCK)], size + MARGIN, 1)[:, :size].astype(bf16)

    def query_terms(cols, size):
        here = lanes(cols, size)
        gq, att = shifted(gq_s, cols, size), shifted(att_s, cols, size)
        dw[:, :C] += mm(gq, xr[:, here], NT)
        dw[:, C : 2 * C] += mm(att, yr[:, here], NT)
        return gq

    def key_terms(cols, size):
        here = lanes(cols, size)
        gk = (gk_s[:, here] * scale).astype(bf16)
        gv = gv_s[:, here].astype(bf16)
        dw[:, 2 * C : 3 * C] += mm(gk, xr[:, here], NT)
        dw[:, 3 * C : 4 * C] += mm(gv, xr[:, here], NT)
        return gk, gv

    def input_terms(cols, size, gq, gk, gv):
        here = lanes(cols, size)
        d = mm(wt[0], gq) + mm(wt[1], gk) + mm(wt[2], gv)
        dout[:, here] = d.astype(bf16)
        bk[me, :, here] = dout[rows_of(me), here]

    def gradients(cols, size):
        gq = query_terms(cols, size)
        gk, gv = key_terms(cols, size)
        input_terms(cols, size, gq, gk, gv)

    def d_copies(cols, size, c):
        return [
            remote(
                dout.at[rows_of(to), lanes(cols, size)], bk.at[me, :, lanes(cols, size)],
                d_send.at[i, c], d_recv.at[i, c], on_mesh(tile, to),
            )
            for i, to in enumerate(others)
        ]

    def chunk(c, carry):
        base = pl.multiple_of(c * CHUNK, CHUNK)
        for copy in chunk_copies(c):
            copy.wait()

        @pl.when(c + 1 < chunks)
        def _():
            start_chunk(c + 1)

        @pl.when(c + 1 == chunks)
        def _():
            for before in range(chunks - 2):
                for copy in d_copies(before * CHUNK, CHUNK, before):
                    copy.start()

        project(pl.ds(pl.multiple_of(base + BLOCK, BLOCK), CHUNK), piece(c))
        gradients(jnp.maximum(c - 1, 0) * CHUNK, CHUNK)
        around = lanes(base, CHUNK + BLOCK)
        q = pltpu.roll(mm(wr[0], xr[:, around]), CHUNK + MARGIN, 1)[:, :CHUNK].astype(bf16)
        g = pltpu.roll(mm(wr[3], yr[:, around]), CHUNK + MARGIN, 1)[:, :CHUNK].astype(bf16)
        scaled = q.astype(f32) * scale2
        high = scaled.astype(bf16)
        low = (scaled - high.astype(f32)).astype(bf16)
        for half in range(2):
            cols = slice(half * BLOCK, (half + 1) * BLOCK)
            for pair in range(pairs):
                u = half * pairs + pair
                for side in range(2):
                    chan = slice((pair * 2 + side) * head_dim, (pair * 2 + side + 1) * head_dim)
                    at = slice(side * head_dim, (side + 1) * head_dim)
                    under = slice(wide_head + side * head_dim, wide_head + (side + 1) * head_dim)
                    lane = slice(side * BLOCK, (side + 1) * BLOCK)
                    qaug[u, at, lane] = high[chan, cols]
                    qaug[u, under, lane] = low[chan, cols]
                    qdiag[u, at, lane] = q[chan, cols]
                    gdiag[u, at, lane] = g[chan, cols]

        units = 2 * pairs
        total, inv, right = {}, {}, {}

        def place(u):
            half, pair = u // pairs, u % pairs
            start = pl.multiple_of(base + half * BLOCK, BLOCK)
            return start, pair, slice(pair * wide_head, (pair + 1) * wide_head)

        def part_rows(part):
            return (slice(0, WINDOW), 0) if part == 0 else (slice(WINDOW, wide), WINDOW)

        def key_rows(u, part):
            return pl.ds(place(u)[0], WINDOW) if part == 0 else slice(near, keys)

        def score(u, part):
            pair = u % pairs
            at, row = part_rows(part)
            left = jnp.concatenate(
                [
                    k_s[key_rows(u, part), pair * BLOCK : (pair + 1) * BLOCK],
                    bias_s[pl.ds(pl.multiple_of((c * 2 + u // pairs) * wide + row, BLOCK), at.stop - row), :],
                ],
                axis=1,
            )
            e = jnp.exp2(mm(left, jnp.concatenate([qaug[u], twice[...]], axis=0)))
            some = jnp.sum(e.reshape((at.stop - row) // 8, 8, 2 * BLOCK), axis=0)
            total[u] = some if part == 0 else total[u] + some
            e_s[u % SLOTS, at, :] = e

        def normal(u, part):
            if part == 0:
                inv[u] = 1.0 / jnp.sum(total[u], axis=0, keepdims=True)
            at, _ = part_rows(part)
            p = e_s[u % SLOTS, at, :] * inv[u]
            e_s[u % SLOTS, at, :] = p
            p_s[u % 3, at, :] = p.astype(bf16)

        def spans(u):
            return (lanes(place(u)[0], WINDOW), slice(0, WINDOW)), (slice(near, keys), slice(WINDOW, wide))

        def attend(u):
            start, pair, chan = place(u)
            att = jnp.zeros((wide_head, 2 * BLOCK), f32)
            for span, at in spans(u):
                att = att + mm(vt_s[chan, span], p_s[u % 3, at, :])
            gd = gdiag[u]
            mean = -jnp.sum(att * gd.astype(f32), axis=0, keepdims=True)
            m0 = mean.astype(bf16).astype(f32)
            m1 = (mean - m0).astype(bf16).astype(f32)
            m2 = mean - m0 - m1
            ids = lax.broadcasted_iota(jnp.int32, (16, 2 * BLOCK), 0)
            rows3 = jnp.where(ids == 0, m0, jnp.where(ids == 1, m1, jnp.where(ids == 2, m2, 0.0))).astype(bf16)
            right[u] = jnp.concatenate([gd, rows3, jnp.zeros((wide_head - 16, 2 * BLOCK), bf16)], axis=0)
            cols = lanes(start + BLOCK, BLOCK)
            first = pair * wide_head
            att_s[first : first + head_dim, cols] = att[:head_dim, :BLOCK]
            att_s[first + head_dim : first + wide_head, cols] = att[head_dim:, BLOCK:]

        def value_grad(u):
            _, _, chan = place(u)
            for span, at in spans(u):
                gv_s[chan, span] += mm(gdiag[u], p_s[u % 3, at, :], NT)

        def dscore(u, part):
            pair = u % pairs
            at, _ = part_rows(part)
            dp = mm(v_s[key_rows(u, part), pair * BLOCK : (pair + 1) * BLOCK], right[u])
            ds_s[u % 3, at, :] = (e_s[u % SLOTS, at, :] * dp).astype(bf16)

        def query_grad(u):
            start, pair, chan = place(u)
            gq = jnp.zeros((wide_head, 2 * BLOCK), f32)
            for span, at in spans(u):
                gq = gq + mm(kt_s[chan, span], ds_s[u % 3, at, :])
            gq = gq * scale
            cols = lanes(start + BLOCK, BLOCK)
            first = pair * wide_head
            gq_s[first : first + head_dim, cols] = gq[:head_dim, :BLOCK]
            gq_s[first + head_dim : first + wide_head, cols] = gq[head_dim:, BLOCK:]

        def key_grad(u):
            _, _, chan = place(u)
            for span, at in spans(u):
                gk_s[chan, span] += mm(qdiag[u], ds_s[u % 3, at, :], NT)

        for i in range(units + 3):
            if 1 <= i < units + 1:
                normal(i - 1, 0)
                normal(i - 1, 1)
            if 0 <= i < units + 0:
                score(i - 0, 0)
                score(i - 0, 1)
            if 1 <= i < units + 1:
                attend(i - 1)
            if 2 <= i < units + 2:
                dscore(i - 2, 0)
                dscore(i - 2, 1)
            if 2 <= i < units + 2:
                value_grad(i - 2)
            if 3 <= i < units + 3:
                query_grad(i - 3)
            if 3 <= i < units + 3:
                key_grad(i - 3)

        return carry

    lax.fori_loop(0, chunks, chunk, 0)

    tail = d_copies((chunks - 2) * CHUNK, CHUNK, chunks - 2) + d_copies((chunks - 1) * CHUNK, CHUNK, chunks - 1) + d_copies(rows, BLOCK, chunks)
    far = slice(near, keys)
    halves = range(0, heads, 2)
    half_cols = 2 * C

    def to_partner(part):
        cols = slice(part * half_cols, (part + 1) * half_cols)
        dwo[part] = (dw[:, cols] * grad_scale).astype(bf16)
        return [
            send(
                dwo.at[part, rows_of((partner + k) % heads)], pr.at[part, i],
                p_send.at[part, i], p_recv.at[part, i], on_mesh(tile, partner),
            )
            for i, k in enumerate(halves)
        ]

    kept, f_copies, r_copies, g_copies = {}, {}, {}, {}

    def to_far(part, copies):
        cols = slice(part * half_cols, (part + 1) * half_cols)
        for copy in copies:
            copy.wait()
        f_copies[part] = []
        for i, k in enumerate(halves):
            value = dw[rows_of((me + k) % heads), cols] * grad_scale + pr[part, i].astype(f32)
            if k:
                fr[part, i - 1] = value.astype(bf16)
                f_copies[part].append(
                    send(
                        fr.at[part, i - 1], fr.at[part, len(halves) - 1 + i - 1],
                        f_send.at[part, i - 1], f_recv.at[part, i - 1], on_mesh(tile, (me + k) % heads),
                    )
                )
            else:
                kept[part] = value

    depth = s1.shape[2]
    blocks = half_cols // 128

    def to_tiles(part):
        for copy in f_copies[part]:
            copy.wait()
        total = kept[part]
        for i in range(len(halves) - 1):
            total = total + fr[part, len(halves) - 1 + i].astype(f32)
        for g in range(groups):
            row, col = (g // blocks) * depth, (g % blocks) * 128
            s1[part, g] = total[row : row + depth, col : col + 128].astype(bf16)
        r_copies[part] = [
            send(s1.at[part, to], rs.at[part, i], r_send.at[part, i], r_recv.at[part, i], on_mesh(to, me))
            for i, to in enumerate(peers)
        ]

    def from_tiles(part):
        for copy in r_copies[part]:
            copy.wait()
        total = s1[part, tile].astype(f32)
        for i in range(groups - 1):
            total = total + rs[part, i].astype(f32)
        totals[part, tile] = total.astype(bf16)
        g_copies[part] = [
            send(
                totals.at[part, tile], totals.at[part, tile],
                g_send.at[part, i], g_recv.at[part, i], on_mesh(to, me),
            )
            for i, to in enumerate(peers)
        ]

    left, size = rows - CHUNK, CHUNK + BLOCK
    gq_left = query_terms(left, size)
    first = to_partner(0)
    gk_left, gv_left = key_terms(left, size)
    gk, gv = key_terms(near, 3 * border)
    second = to_partner(1)
    to_far(0, first)
    to_far(1, second)
    input_terms(left, size, gq_left, gk_left, gv_left)
    db[...] = (mm(wt[1], gk) + mm(wt[2], gv)).astype(bf16)
    b_copies = [
        send(db.at[rows_of(to), :], br.at[i], b_send.at[i], b_recv.at[i], on_mesh(tile, to))
        for i, to in enumerate(others)
    ]
    for copy in tail:
        copy.start()
    to_tiles(0)
    to_tiles(1)
    for copy in b_copies:
        copy.wait()
    edge_sum = db[rows_of(me), :].astype(f32)
    for i in range(heads - 1):
        edge_sum = edge_sum + br[i].astype(f32)
    mine[...] = edge_sum.astype(bf16)
    a_copies = [
        send(
            mine.at[:, p * border : (p + 1) * border], answers.at[p],
            a_send.at[p], a_recv.at[p], on_mesh((tile + groups - offsets[p]) % groups, me),
        )
        for p in range(3)
    ]
    from_tiles(0)
    from_tiles(1)

    for copy in a_copies:
        copy.wait()
    for copy in tail:
        copy.wait()

    def d_wait(c, carry):
        for copy in d_copies(c * CHUNK, CHUNK, c):
            copy.wait()
        return carry

    lax.fori_loop(0, chunks - 2, d_wait, 0)
    back = jnp.concatenate([answers[p] for p in range(3)], axis=1)
    for h in range(heads):
        for i in range(rows // CHUNK):
            cols = slice(h * rows + i * CHUNK, h * rows + (i + 1) * CHUNK)
            value = dy[:, cols].astype(f32) + bk[h, :, i * CHUNK : (i + 1) * CHUNK].astype(f32)
            value = value + mm(back, chosen[cols, :], NT)
            if i == 0:
                edge = bk[(h - 1) % heads, :, rows:near].astype(f32)
                value = value + jnp.concatenate([edge, jnp.zeros((share, CHUNK - BLOCK), f32)], axis=1)
            result[:, cols] = value
    out_copy = pltpu.make_async_copy(result, d_out, out_sem.at[0])
    out_copy.start()

    for part in range(2):
        for copy in g_copies[part]:
            copy.wait()
        for g in range(groups):
            row, col = (g // blocks) * depth, (g % blocks) * 128
            lane = col % C
            value = totals[part, g].astype(f32)
            if part == 0 and col >= C:
                gout_out[row : row + depth, lane : lane + 128] = value
            else:
                gqkv_out[part + col // C, row : row + depth, lane : lane + 128] = value
    out_copy.wait()


def local(tokens, grad_in, w_qkv, w_out, neighbors, send_rows):
    groups = lax.axis_size("tile")
    heads = lax.axis_size("head")
    border = send_rows.shape[2]
    share, full_rows = tokens.shape
    rows = full_rows // heads
    near = rows + BLOCK
    keys = near + 3 * border
    wide = WINDOW + 3 * border
    bf16, f32 = jnp.bfloat16, jnp.float32
    grad_scale = 1.0 / math.sqrt(full_rows * groups)
    vm = pltpu.VMEM
    dma = pltpu.SemaphoreType.DMA
    far = (heads - 1) // 2
    others, peers = heads - 1, groups - 1
    depth = share * 2 * C // 128 // groups
    chunks = rows // CHUNK
    units = HEADS
    any_ = pl.BlockSpec(memory_space=pl.ANY)
    in_vm = pl.BlockSpec(memory_space=vm)
    return pl.pallas_call(
        functools.partial(attention_body, groups, heads, share, border, rows, grad_scale),
        out_shape=(
            jax.ShapeDtypeStruct((share, full_rows), f32),
            jax.ShapeDtypeStruct((3, share, C), f32),
            jax.ShapeDtypeStruct((share, C), f32),
        ),
        in_specs=[any_] * 6,
        out_specs=[any_, in_vm, in_vm],
        scratch_shapes=[
            vm((share, full_rows), bf16),
            vm((share, full_rows), bf16),
            vm((C, keys), bf16),
            vm((C, near), bf16),
            vm((4, C, C), bf16),
            vm((2 * C, C), bf16),
            vm((2 * C, C), bf16),
            vm((3, C, C), bf16),
            vm((full_rows, 3 * border), bf16),
            vm((share, 3 * border), bf16),
            vm((rows // BLOCK * wide, BLOCK), bf16),
            vm((BLOCK, 2 * BLOCK), bf16),
            vm((keys, 2 * C), bf16),
            vm((keys, 2 * C), bf16),
            vm((C, keys), bf16),
            vm((C, keys), bf16),
            vm((units, BLOCK, 2 * BLOCK), bf16),
            vm((units, 2 * C // HEADS, 2 * BLOCK), bf16),
            vm((units, 2 * C // HEADS, 2 * BLOCK), bf16),
            vm((SLOTS, wide, 2 * BLOCK), f32),
            vm((3, wide, 2 * BLOCK), bf16),
            vm((3, wide, 2 * BLOCK), bf16),
            vm((C, keys), f32),
            vm((C, keys), f32),
            vm((C, near + BLOCK), f32),
            vm((C, near + BLOCK), f32),
            vm((C, 4 * C), f32),
            vm((2, C, 2 * C), bf16),
            vm((2, heads // 2, share, 2 * C), bf16),
            vm((2, 2 * far, share, 2 * C), bf16),
            vm((2, groups, depth, 128), bf16),
            vm((2, peers, depth, 128), bf16),
            vm((2, groups, depth, 128), bf16),
            vm((C, near), bf16),
            vm((heads, share, near), bf16),
            vm((C, 3 * border), bf16),
            vm((3, share, border), bf16),
            vm((share, full_rows), f32),
            vm((heads - 1, share, 3 * border), bf16),
            vm((NBR, full_rows), jnp.int32),
            vm((1, 3, border), jnp.int32),
        ]
        + [dma((10,))]
        + [dma((2, far + 1))] * 2
        + [dma((far,))] * 2
        + [dma((others,))] * 4
        + [dma((others, chunks))] * 4
        + [dma((3, far + 2))] * 2
        + [dma((far,))] * 2
        + [dma((others, chunks + 1))] * 2
        + [dma((others,))] * 2
        + [dma((3,))] * 2
        + [dma((2, heads // 2))] * 2
        + [dma((2, far))] * 2
        + [dma((2, peers))] * 4
        + [dma((1,))],
        compiler_params=pltpu.CompilerParams(
            collective_id=0, has_side_effects=True, vmem_limit_bytes=56 * 1024 * 1024
        ),
        name="attend",
    )(tokens, grad_in, w_qkv, w_out, neighbors, send_rows)


def solution(mesh):
    return jax.shard_map(
        local,
        mesh=mesh,
        in_specs=(
            P("head", "tile"),
            P("head", "tile"),
            P(None, "head", None),
            P("head", None),
            P(None, "tile"),
            P("tile", None, None),
        ),
        out_specs=(P("head", "tile"), P(None, "head", None), P("head", None)),
        check_vma=False,
    )
```

```python
import functools
import math

import jax
import jax.numpy as jnp
from jax import lax
from jax.experimental import pallas as pl
from jax.experimental.pallas import tpu as pltpu
from jax.sharding import PartitionSpec as P

C = 256
HEADS = 8
NBR = 9
MARGIN = 64
BLOCK = 2 * MARGIN
WINDOW = 2 * BLOCK
CHUNK = 2 * BLOCK
NEVER = -1.0e30
SLOTS = 4

NN = (((1,), (0,)), ((), ()))
NT = (((1,), (1,)), ((), ()))


def mm(a, b, dims=NN):
    return lax.dot_general(a, b, dims, preferred_element_type=jnp.float32)


def on_mesh(tile, head):
    return {"tile": tile, "head": head}


def greet(peers):
    barrier = pltpu.get_barrier_semaphore()
    for peer in peers:
        pl.semaphore_signal(barrier, inc=1, device_id=peer, device_id_type=pl.DeviceIdType.MESH)
    pl.semaphore_wait(barrier, len(peers))


def remote(src, dst, send_sem, recv_sem, peer):
    return pltpu.make_async_remote_copy(
        src_ref=src,
        dst_ref=dst,
        send_sem=send_sem,
        recv_sem=recv_sem,
        device_id=peer,
        device_id_type=pl.DeviceIdType.MESH,
    )


def send(*args):
    copy = remote(*args)
    copy.start()
    return copy


def attention_body(
    groups, heads, share, border, rows, grad_scale,
    tokens, grad_in, w_qkv, w_out, neighbors_in, send_rows_in,
    d_out, totals_out,
    tok, xr, yr, wr, wkd, wvp, wt, chosen, mine, bias_s, twice,
    k_s, v_s, kt_s, vt_s, qaug, qdiag, gdiag, e_s, p_s, ds_s,
    gk_s, gv_s, att_s, gq_s, dw, dwo, pr, fr, s1, rs, totals,
    dout, bk, db, answers, result, br, neighbors, send_rows,
    local_sem, w_send, w_recv, wf_send, wf_recv, xp_send, xp_recv, yp_send, yp_recv,
    x_send, x_recv, y_send, y_recv, e_send, e_recv, ef_send, ef_recv,
    d_send, d_recv, b_send, b_recv, a_send, a_recv, p_send, p_recv, f_send, f_recv,
    r_send, r_recv, g_send, g_recv, out_sem,
):
    head_dim = C // HEADS
    wide_head = 2 * head_dim
    pairs = HEADS // 2
    scale = 1.0 / math.sqrt(head_dim)
    scale2 = scale / math.log(2.0)
    near = rows + BLOCK
    keys = near + 3 * border
    wide = WINDOW + 3 * border
    tiles = wide // BLOCK
    full_rows = rows * heads
    chunks = rows // CHUNK
    bf16, f32 = jnp.bfloat16, jnp.float32
    tile, me = lax.axis_index("tile"), lax.axis_index("head")
    offsets = (1, groups - 1, groups // 2)
    partner = (me // 2) * 2 + 1 - me % 2
    steps = range(2, heads, 2)
    others = [(me + k) % heads for k in range(1, heads)]
    peers = [(tile + k) % groups for k in range(1, groups)]

    def rows_of(index):
        return pl.ds(pl.multiple_of(index * share, share), share)

    def lanes(start, size):
        return pl.ds(pl.multiple_of(start, BLOCK), size)

    greet(
        [on_mesh(tile, to) for to in others]
        + [on_mesh(to, me) for to in peers]
        + [on_mesh((tile + offset) % groups, to) for offset in offsets for to in others]
    )

    locals_ = [pltpu.make_async_copy(tokens, tok, local_sem.at[0])]
    pairs_of = ((tokens, xr), (grad_in, yr))
    own = lanes(me * rows, rows)
    after = lanes(((me + 1) % heads) * rows, BLOCK)
    for i, (src, dst) in enumerate(pairs_of):
        locals_.append(pltpu.make_async_copy(src.at[:, own], dst.at[rows_of(me), 0:rows], local_sem.at[1 + 2 * i]))
        locals_.append(
            pltpu.make_async_copy(src.at[:, after], dst.at[rows_of(me), rows:near], local_sem.at[2 + 2 * i])
        )
    locals_.append(pltpu.make_async_copy(w_qkv, wr.at[0:3, rows_of(me), :], local_sem.at[5]))
    locals_.append(pltpu.make_async_copy(w_out, wr.at[3, rows_of(me), :], local_sem.at[6]))
    locals_.append(pltpu.make_async_copy(neighbors_in, neighbors, local_sem.at[7]))
    rows_copy = pltpu.make_async_copy(send_rows_in, send_rows, local_sem.at[8])
    rows_copy.start()
    for copy in locals_:
        copy.start()

    w_copies = []
    for i, to in enumerate([(me + k) % heads for k in steps] + [partner]):
        w_copies.append(
            [
                send(w_qkv, wr.at[0:3, rows_of(me), :], w_send.at[0, i], w_recv.at[0, i], on_mesh(tile, to)),
                send(w_out, wr.at[3, rows_of(me), :], w_send.at[1, i], w_recv.at[1, i], on_mesh(tile, to)),
            ]
        )
    def piece(c):
        return lanes(BLOCK + c * CHUNK, CHUNK)

    def start_chunk(c):
        first = BLOCK + c * CHUNK
        for i, to in enumerate(others):
            for src, dst, ss, rr in ((tokens, xr, x_send, x_recv), (grad_in, yr, y_send, y_recv)):
                for at in (first, first + BLOCK):
                    frm = (to * rows + at) % full_rows
                    send(
                        src.at[:, lanes(frm, BLOCK)], dst.at[rows_of(me), lanes(at, BLOCK)],
                        ss.at[i, c], rr.at[i, c], on_mesh(tile, to),
                    )

    def chunk_copies(c):
        copies = []
        for i, to in enumerate(others):
            for src, dst, ss, rr in ((tokens, xr, x_send, x_recv), (grad_in, yr, y_send, y_recv)):
                copies.append(
                    remote(
                        src.at[:, 0:CHUNK], dst.at[rows_of(me), piece(c)],
                        ss.at[i, c], rr.at[i, c], on_mesh(tile, to),
                    )
                )
        return copies

    rows_copy.wait()
    flat = jnp.concatenate([send_rows[0, p : p + 1, :] for p in range(3)], axis=1)

    def choose(i, carry):
        ids = lax.broadcasted_iota(jnp.int32, (CHUNK, 3 * border), 0) + i * CHUNK
        at = pl.ds(pl.multiple_of(i * CHUNK, CHUNK), CHUNK)
        chosen[at, :] = jnp.where(ids == flat, 1.0, 0.0).astype(bf16)
        return carry

    lax.fori_loop(0, full_rows // CHUNK, choose, 0)
    locals_[0].wait()
    mine[...] = mm(tok[...], chosen[...]).astype(bf16)
    e_copies = []
    for p in range(3):
        there = (tile + offsets[p]) % groups
        cols = slice(near + p * border, near + (p + 1) * border)
        for i, to in enumerate([(me + k) % heads for k in steps] + [me, partner]):
            e_copies.append(
                send(
                    mine.at[:, p * border : (p + 1) * border], xr.at[rows_of(me), cols],
                    e_send.at[p, i], e_recv.at[p, i], on_mesh(there, to),
                )
            )

    moving = []
    for i, to in enumerate(others):
        for src, dst, ss, rr in ((tokens, xr, xp_send, xp_recv), (grad_in, yr, yp_send, yp_recv)):
            moving.append(
                send(src.at[:, lanes(to * rows, BLOCK)], dst.at[rows_of(me), 0:BLOCK], ss.at[i], rr.at[i], on_mesh(tile, to))
            )

    start_chunk(0)

    locals_[7].wait()
    def mask(b, carry):
        start = pl.multiple_of(b * BLOCK, BLOCK)
        here = me * rows + start
        one = neighbors[:, lanes(here, BLOCK)]
        two = neighbors[:, lanes((here + BLOCK) % full_rows, BLOCK)]
        ring = jnp.concatenate([one[:, MARGIN:], two[:, :MARGIN]], axis=1)
        along = ring - me * rows
        along = jnp.where(along < 0, along + full_rows, along)
        picks = jnp.where(ring < full_rows, along - start, ring - full_rows + WINDOW)
        for t in range(tiles):
            ids = lax.broadcasted_iota(jnp.int32, (BLOCK, BLOCK), 0) + t * BLOCK
            count = jnp.zeros((BLOCK, BLOCK), f32)
            for j in range(NBR):
                count = count + jnp.where(ids == picks[j : j + 1, :], 1.0, 0.0)
            bias = jnp.where(count > 0.0, jnp.log2(jnp.maximum(count, 1.0)), NEVER)
            bias_s[pl.ds(pl.multiple_of(b * wide + t * BLOCK, BLOCK), BLOCK), :] = bias.astype(bf16)
        return carry

    lax.fori_loop(0, rows // BLOCK, mask, 0)
    qaug[...] = jnp.zeros_like(qaug)
    qdiag[...] = jnp.zeros_like(qdiag)
    gdiag[...] = jnp.zeros_like(gdiag)
    gk_s[...] = jnp.zeros_like(gk_s)
    gv_s[...] = jnp.zeros_like(gv_s)
    dw[...] = jnp.zeros_like(dw)
    att_s[...] = jnp.zeros_like(att_s)
    gq_s[...] = jnp.zeros_like(gq_s)
    diag = jnp.where(
        lax.broadcasted_iota(jnp.int32, (BLOCK, BLOCK), 0) == lax.broadcasted_iota(jnp.int32, (BLOCK, BLOCK), 1), 1.0, 0.0
    ).astype(bf16)
    twice[:, :BLOCK] = diag
    twice[:, BLOCK:] = diag
    wvp[...] = jnp.zeros_like(wvp)

    last = []
    for i, k in enumerate(steps):
        for copy in w_copies[i]:
            copy.wait()
        block_ref = wr.at[:, rows_of((me + heads - k) % heads), :]
        last.append(send(block_ref, block_ref, wf_send.at[i], wf_recv.at[i], on_mesh(tile, partner)))
    for copy in w_copies[len(steps)]:
        copy.wait()
    for copy in e_copies:
        copy.wait()
    for i, k in enumerate(steps):
        block_ref = xr.at[rows_of((me + heads - k) % heads), near:keys]
        last.append(send(block_ref, block_ref, ef_send.at[i], ef_recv.at[i], on_mesh(tile, partner)))
    for copy in locals_[1:7]:
        copy.wait()
    for i in range(len(steps)):
        last[i].wait()
    for t in range(3):
        wt[t] = wr[t].T
    for pair in range(pairs):
        chan = slice(pair * wide_head, (pair + 1) * wide_head)
        base = pair * 2 * wide_head
        wkd[base : base + wide_head, :] = wr[1, chan, :]
        wkd[base + wide_head : base + 2 * wide_head, :] = wr[1, chan, :]
        wvp[base : base + wide_head, :] = wr[2, chan, :]

    lane_id = lax.broadcasted_iota(jnp.int32, (1, 2 * C), 1) % (2 * wide_head)
    ones = jnp.where((lane_id >= wide_head) & (lane_id < wide_head + 3), 1.0, 0.0)

    def project(at_rows, at_cols):
        x = xr[:, at_cols]
        xt = x.T
        k_s[at_rows, :] = mm(xt, wkd[...], NT).astype(bf16)
        v_s[at_rows, :] = (mm(xt, wvp[...], NT) + ones).astype(bf16)
        kt_s[:, at_cols] = mm(wr[1], x).astype(bf16)
        vt_s[:, at_cols] = mm(wr[2], x).astype(bf16)

    for copy in moving:
        copy.wait()
    project(slice(0, BLOCK), slice(0, BLOCK))
    for i in range(len(steps)):
        last[len(steps) + i].wait()
    project(slice(near, keys), slice(near, keys))

    def shifted(ref, cols, size):
        return pltpu.roll(ref[:, lanes(cols, size + BLOCK)], size + MARGIN, 1)[:, :size].astype(bf16)

    def query_terms(cols, size):
        here = lanes(cols, size)
        gq, att = shifted(gq_s, cols, size), shifted(att_s, cols, size)
        dw[:, :C] += mm(gq, xr[:, here], NT)
        dw[:, C : 2 * C] += mm(att, yr[:, here], NT)
        return gq

    def key_terms(cols, size):
        here = lanes(cols, size)
        gk = (gk_s[:, here] * scale).astype(bf16)
        gv = gv_s[:, here].astype(bf16)
        dw[:, 2 * C : 3 * C] += mm(gk, xr[:, here], NT)
        dw[:, 3 * C : 4 * C] += mm(gv, xr[:, here], NT)
        return gk, gv

    def input_terms(cols, size, gq, gk, gv):
        here = lanes(cols, size)
        d = mm(wt[0], gq) + mm(wt[1], gk) + mm(wt[2], gv)
        dout[:, here] = d.astype(bf16)
        bk[me, :, here] = dout[rows_of(me), here]

    def gradients(cols, size):
        gq = query_terms(cols, size)
        gk, gv = key_terms(cols, size)
        input_terms(cols, size, gq, gk, gv)

    def d_copies(cols, size, c):
        return [
            remote(
                dout.at[rows_of(to), lanes(cols, size)], bk.at[me, :, lanes(cols, size)],
                d_send.at[i, c], d_recv.at[i, c], on_mesh(tile, to),
            )
            for i, to in enumerate(others)
        ]

    def chunk(c, carry):
        base = pl.multiple_of(c * CHUNK, CHUNK)
        for copy in chunk_copies(c):
            copy.wait()

        @pl.when(c + 1 < chunks)
        def _():
            start_chunk(c + 1)

        @pl.when(c + 1 == chunks)
        def _():
            for before in range(chunks - 2):
                for copy in d_copies(before * CHUNK, CHUNK, before):
                    copy.start()

        project(pl.ds(pl.multiple_of(base + BLOCK, BLOCK), CHUNK), piece(c))
        gradients(jnp.maximum(c - 1, 0) * CHUNK, CHUNK)
        around = lanes(base, CHUNK + BLOCK)
        q = pltpu.roll(mm(wr[0], xr[:, around]), CHUNK + MARGIN, 1)[:, :CHUNK].astype(bf16)
        g = pltpu.roll(mm(wr[3], yr[:, around]), CHUNK + MARGIN, 1)[:, :CHUNK].astype(bf16)
        scaled = q.astype(f32) * scale2
        high = scaled.astype(bf16)
        low = (scaled - high.astype(f32)).astype(bf16)
        for half in range(2):
            cols = slice(half * BLOCK, (half + 1) * BLOCK)
            for pair in range(pairs):
                u = half * pairs + pair
                for side in range(2):
                    chan = slice((pair * 2 + side) * head_dim, (pair * 2 + side + 1) * head_dim)
                    at = slice(side * head_dim, (side + 1) * head_dim)
                    under = slice(wide_head + side * head_dim, wide_head + (side + 1) * head_dim)
                    lane = slice(side * BLOCK, (side + 1) * BLOCK)
                    qaug[u, at, lane] = high[chan, cols]
                    qaug[u, under, lane] = low[chan, cols]
                    qdiag[u, at, lane] = q[chan, cols]
                    gdiag[u, at, lane] = g[chan, cols]

        units = 2 * pairs
        total, inv, right = {}, {}, {}

        def place(u):
            half, pair = u // pairs, u % pairs
            start = pl.multiple_of(base + half * BLOCK, BLOCK)
            return start, pair, slice(pair * wide_head, (pair + 1) * wide_head)

        def part_rows(part):
            return (slice(0, WINDOW), 0) if part == 0 else (slice(WINDOW, wide), WINDOW)

        def key_rows(u, part):
            return pl.ds(place(u)[0], WINDOW) if part == 0 else slice(near, keys)

        def score(u, part):
            pair = u % pairs
            at, row = part_rows(part)
            left = jnp.concatenate(
                [
                    k_s[key_rows(u, part), pair * BLOCK : (pair + 1) * BLOCK],
                    bias_s[pl.ds(pl.multiple_of((c * 2 + u // pairs) * wide + row, BLOCK), at.stop - row), :],
                ],
                axis=1,
            )
            e = jnp.exp2(mm(left, jnp.concatenate([qaug[u], twice[...]], axis=0)))
            some = jnp.sum(e.reshape((at.stop - row) // 8, 8, 2 * BLOCK), axis=0)
            total[u] = some if part == 0 else total[u] + some
            e_s[u % SLOTS, at, :] = e

        def normal(u, part):
            if part == 0:
                inv[u] = 1.0 / jnp.sum(total[u], axis=0, keepdims=True)
            at, _ = part_rows(part)
            p = e_s[u % SLOTS, at, :] * inv[u]
            e_s[u % SLOTS, at, :] = p
            p_s[u % 3, at, :] = p.astype(bf16)

        def spans(u):
            return (lanes(place(u)[0], WINDOW), slice(0, WINDOW)), (slice(near, keys), slice(WINDOW, wide))

        def attend(u):
            start, pair, chan = place(u)
            att = jnp.zeros((wide_head, 2 * BLOCK), f32)
            for span, at in spans(u):
                att = att + mm(vt_s[chan, span], p_s[u % 3, at, :])
            gd = gdiag[u]
            mean = -jnp.sum(att * gd.astype(f32), axis=0, keepdims=True)
            m0 = mean.astype(bf16).astype(f32)
            m1 = (mean - m0).astype(bf16).astype(f32)
            m2 = mean - m0 - m1
            ids = lax.broadcasted_iota(jnp.int32, (16, 2 * BLOCK), 0)
            rows3 = jnp.where(ids == 0, m0, jnp.where(ids == 1, m1, jnp.where(ids == 2, m2, 0.0))).astype(bf16)
            right[u] = jnp.concatenate([gd, rows3, jnp.zeros((wide_head - 16, 2 * BLOCK), bf16)], axis=0)
            cols = lanes(start + BLOCK, BLOCK)
            first = pair * wide_head
            att_s[first : first + head_dim, cols] = att[:head_dim, :BLOCK]
            att_s[first + head_dim : first + wide_head, cols] = att[head_dim:, BLOCK:]

        def value_grad(u):
            _, _, chan = place(u)
            for span, at in spans(u):
                gv_s[chan, span] += mm(gdiag[u], p_s[u % 3, at, :], NT)

        def dscore(u, part):
            pair = u % pairs
            at, _ = part_rows(part)
            dp = mm(v_s[key_rows(u, part), pair * BLOCK : (pair + 1) * BLOCK], right[u])
            ds_s[u % 3, at, :] = (e_s[u % SLOTS, at, :] * dp).astype(bf16)

        def query_grad(u):
            start, pair, chan = place(u)
            gq = jnp.zeros((wide_head, 2 * BLOCK), f32)
            for span, at in spans(u):
                gq = gq + mm(kt_s[chan, span], ds_s[u % 3, at, :])
            gq = gq * scale
            cols = lanes(start + BLOCK, BLOCK)
            first = pair * wide_head
            gq_s[first : first + head_dim, cols] = gq[:head_dim, :BLOCK]
            gq_s[first + head_dim : first + wide_head, cols] = gq[head_dim:, BLOCK:]

        def key_grad(u):
            _, _, chan = place(u)
            for span, at in spans(u):
                gk_s[chan, span] += mm(qdiag[u], ds_s[u % 3, at, :], NT)

        for i in range(units + 3):
            if 1 <= i < units + 1:
                normal(i - 1, 0)
                normal(i - 1, 1)
            if 0 <= i < units + 0:
                score(i - 0, 0)
                score(i - 0, 1)
            if 1 <= i < units + 1:
                attend(i - 1)
            if 2 <= i < units + 2:
                dscore(i - 2, 0)
                dscore(i - 2, 1)
            if 2 <= i < units + 2:
                value_grad(i - 2)
            if 3 <= i < units + 3:
                query_grad(i - 3)
            if 3 <= i < units + 3:
                key_grad(i - 3)

        return carry

    lax.fori_loop(0, chunks, chunk, 0)

    tail = d_copies((chunks - 2) * CHUNK, CHUNK, chunks - 2) + d_copies((chunks - 1) * CHUNK, CHUNK, chunks - 1) + d_copies(rows, BLOCK, chunks)
    far = slice(near, keys)
    halves = range(0, heads, 2)
    half_cols = 2 * C

    def to_partner(part):
        cols = slice(part * half_cols, (part + 1) * half_cols)
        dwo[part] = (dw[:, cols] * grad_scale).astype(bf16)
        return [
            send(
                dwo.at[part, rows_of((partner + k) % heads)], pr.at[part, i],
                p_send.at[part, i], p_recv.at[part, i], on_mesh(tile, partner),
            )
            for i, k in enumerate(halves)
        ]

    kept, f_copies, r_copies, g_copies = {}, {}, {}, {}

    def to_far(part, copies):
        cols = slice(part * half_cols, (part + 1) * half_cols)
        for copy in copies:
            copy.wait()
        f_copies[part] = []
        for i, k in enumerate(halves):
            value = dw[rows_of((me + k) % heads), cols] * grad_scale + pr[part, i].astype(f32)
            if k:
                fr[part, i - 1] = value.astype(bf16)
                f_copies[part].append(
                    send(
                        fr.at[part, i - 1], fr.at[part, len(halves) - 1 + i - 1],
                        f_send.at[part, i - 1], f_recv.at[part, i - 1], on_mesh(tile, (me + k) % heads),
                    )
                )
            else:
                kept[part] = value

    depth = s1.shape[2]
    blocks = half_cols // 128

    def to_tiles(part):
        for copy in f_copies[part]:
            copy.wait()
        total = kept[part]
        for i in range(len(halves) - 1):
            total = total + fr[part, len(halves) - 1 + i].astype(f32)
        for g in range(groups):
            row, col = (g // blocks) * depth, (g % blocks) * 128
            s1[part, g] = total[row : row + depth, col : col + 128].astype(bf16)
        r_copies[part] = [
            send(s1.at[part, to], rs.at[part, i], r_send.at[part, i], r_recv.at[part, i], on_mesh(to, me))
            for i, to in enumerate(peers)
        ]

    def from_tiles(part):
        for copy in r_copies[part]:
            copy.wait()
        total = s1[part, tile].astype(f32)
        for i in range(groups - 1):
            total = total + rs[part, i].astype(f32)
        totals[part, tile] = total.astype(bf16)
        g_copies[part] = [
            send(
                totals.at[part, tile], totals.at[part, tile],
                g_send.at[part, i], g_recv.at[part, i], on_mesh(to, me),
            )
            for i, to in enumerate(peers)
        ]

    left, size = rows - CHUNK, CHUNK + BLOCK
    gq_left = query_terms(left, size)
    first = to_partner(0)
    gk_left, gv_left = key_terms(left, size)
    gk, gv = key_terms(near, 3 * border)
    second = to_partner(1)
    to_far(0, first)
    to_far(1, second)
    input_terms(left, size, gq_left, gk_left, gv_left)
    db[...] = (mm(wt[1], gk) + mm(wt[2], gv)).astype(bf16)
    b_copies = [
        send(db.at[rows_of(to), :], br.at[i], b_send.at[i], b_recv.at[i], on_mesh(tile, to))
        for i, to in enumerate(others)
    ]
    for copy in tail:
        copy.start()
    to_tiles(0)
    to_tiles(1)
    for copy in b_copies:
        copy.wait()
    edge_sum = db[rows_of(me), :].astype(f32)
    for i in range(heads - 1):
        edge_sum = edge_sum + br[i].astype(f32)
    mine[...] = edge_sum.astype(bf16)
    a_copies = [
        send(
            mine.at[:, p * border : (p + 1) * border], answers.at[p],
            a_send.at[p], a_recv.at[p], on_mesh((tile + groups - offsets[p]) % groups, me),
        )
        for p in range(3)
    ]
    from_tiles(0)
    from_tiles(1)

    for copy in a_copies:
        copy.wait()
    for copy in tail:
        copy.wait()

    def d_wait(c, carry):
        for copy in d_copies(c * CHUNK, CHUNK, c):
            copy.wait()
        return carry

    lax.fori_loop(0, chunks - 2, d_wait, 0)
    back = jnp.concatenate([answers[p] for p in range(3)], axis=1)
    for h in range(heads):
        for i in range(rows // CHUNK):
            cols = slice(h * rows + i * CHUNK, h * rows + (i + 1) * CHUNK)
            value = bk[h, :, i * CHUNK : (i + 1) * CHUNK].astype(f32)
            value = value + mm(back, chosen[cols, :], NT)
            if i == 0:
                edge = bk[(h - 1) % heads, :, rows:near].astype(f32)
                value = value + jnp.concatenate([edge, jnp.zeros((share, CHUNK - BLOCK), f32)], axis=1)
            result[:, cols] = value.astype(bf16)
    out_copy = pltpu.make_async_copy(result, d_out, out_sem.at[0])
    out_copy.start()

    for part in range(2):
        for copy in g_copies[part]:
            copy.wait()
    totals_out[...] = totals[...]
    out_copy.wait()


def finish_body(
    grad_in, d_sum, totals_in, d_out, gqkv_to, gout_to,
    dy, summed, result, totals, gqkv_out, gout_out, in_sem, sum_sem, out_sem, small_sem,
):
    parts = in_sem.shape[0]
    width = dy.shape[1] // parts
    _, groups, depth, _ = totals.shape
    blocks = 2 * C // 128
    cols = [slice(i * width, (i + 1) * width) for i in range(parts)]
    first = pltpu.make_async_copy(totals_in, totals, small_sem.at[0])
    first.start()
    copies = []
    for i in range(parts):
        copies.append(
            (
                pltpu.make_async_copy(grad_in.at[:, cols[i]], dy.at[:, cols[i]], in_sem.at[i]),
                pltpu.make_async_copy(d_sum.at[:, cols[i]], summed.at[:, cols[i]], sum_sem.at[i]),
            )
        )
        for copy in copies[-1]:
            copy.start()
    first.wait()
    for part in range(2):
        for g in range(groups):
            row, col = (g // blocks) * depth, (g % blocks) * 128
            lane = col % C
            value = totals[part, g].astype(jnp.float32)
            if part == 0 and col >= C:
                gout_out[row : row + depth, lane : lane + 128] = value
            else:
                gqkv_out[part + col // C, row : row + depth, lane : lane + 128] = value
    outs = [
        pltpu.make_async_copy(gqkv_out, gqkv_to, small_sem.at[1]),
        pltpu.make_async_copy(gout_out, gout_to, small_sem.at[2]),
    ]
    for copy in outs:
        copy.start()
    for i in range(parts):
        for copy in copies[i]:
            copy.wait()
        result[:, cols[i]] = dy[:, cols[i]].astype(jnp.float32) + summed[:, cols[i]].astype(jnp.float32)
        outs.append(pltpu.make_async_copy(result.at[:, cols[i]], d_out.at[:, cols[i]], out_sem.at[i]))
        outs[-1].start()
    for copy in outs:
        copy.wait()


def local(tokens, grad_in, w_qkv, w_out, neighbors, send_rows):
    groups = lax.axis_size("tile")
    heads = lax.axis_size("head")
    border = send_rows.shape[2]
    share, full_rows = tokens.shape
    rows = full_rows // heads
    near = rows + BLOCK
    keys = near + 3 * border
    wide = WINDOW + 3 * border
    bf16, f32 = jnp.bfloat16, jnp.float32
    grad_scale = 1.0 / math.sqrt(full_rows * groups)
    vm = pltpu.VMEM
    dma = pltpu.SemaphoreType.DMA
    far = (heads - 1) // 2
    others, peers = heads - 1, groups - 1
    depth = share * 2 * C // 128 // groups
    chunks = rows // CHUNK
    units = HEADS
    any_ = pl.BlockSpec(memory_space=pl.ANY)
    in_vm = pl.BlockSpec(memory_space=vm)
    d_sum, totals = pl.pallas_call(
        functools.partial(attention_body, groups, heads, share, border, rows, grad_scale),
        out_shape=(
            jax.ShapeDtypeStruct((share, full_rows), bf16),
            jax.ShapeDtypeStruct((2, groups, depth, 128), bf16),
        ),
        in_specs=[any_] * 6,
        out_specs=[any_, in_vm],
        scratch_shapes=[
            vm((share, full_rows), bf16),
            vm((C, keys), bf16),
            vm((C, near), bf16),
            vm((4, C, C), bf16),
            vm((2 * C, C), bf16),
            vm((2 * C, C), bf16),
            vm((3, C, C), bf16),
            vm((full_rows, 3 * border), bf16),
            vm((share, 3 * border), bf16),
            vm((rows // BLOCK * wide, BLOCK), bf16),
            vm((BLOCK, 2 * BLOCK), bf16),
            vm((keys, 2 * C), bf16),
            vm((keys, 2 * C), bf16),
            vm((C, keys), bf16),
            vm((C, keys), bf16),
            vm((units, BLOCK, 2 * BLOCK), bf16),
            vm((units, 2 * C // HEADS, 2 * BLOCK), bf16),
            vm((units, 2 * C // HEADS, 2 * BLOCK), bf16),
            vm((SLOTS, wide, 2 * BLOCK), f32),
            vm((3, wide, 2 * BLOCK), bf16),
            vm((3, wide, 2 * BLOCK), bf16),
            vm((C, keys), f32),
            vm((C, keys), f32),
            vm((C, near + BLOCK), f32),
            vm((C, near + BLOCK), f32),
            vm((C, 4 * C), f32),
            vm((2, C, 2 * C), bf16),
            vm((2, heads // 2, share, 2 * C), bf16),
            vm((2, 2 * far, share, 2 * C), bf16),
            vm((2, groups, depth, 128), bf16),
            vm((2, peers, depth, 128), bf16),
            vm((2, groups, depth, 128), bf16),
            vm((C, near), bf16),
            vm((heads, share, near), bf16),
            vm((C, 3 * border), bf16),
            vm((3, share, border), bf16),
            vm((share, full_rows), bf16),
            vm((heads - 1, share, 3 * border), bf16),
            vm((NBR, full_rows), jnp.int32),
            vm((1, 3, border), jnp.int32),
        ]
        + [dma((9,))]
        + [dma((2, far + 1))] * 2
        + [dma((far,))] * 2
        + [dma((others,))] * 4
        + [dma((others, chunks))] * 4
        + [dma((3, far + 2))] * 2
        + [dma((far,))] * 2
        + [dma((others, chunks + 1))] * 2
        + [dma((others,))] * 2
        + [dma((3,))] * 2
        + [dma((2, heads // 2))] * 2
        + [dma((2, far))] * 2
        + [dma((2, peers))] * 4
        + [dma((1,))],
        compiler_params=pltpu.CompilerParams(
            collective_id=0, has_side_effects=True, vmem_limit_bytes=56 * 1024 * 1024
        ),
        name="attend",
    )(tokens, grad_in, w_qkv, w_out, neighbors, send_rows)
    parts = 4
    return pl.pallas_call(
        finish_body,
        out_shape=(
            jax.ShapeDtypeStruct((share, full_rows), f32),
            jax.ShapeDtypeStruct((3, share, C), f32),
            jax.ShapeDtypeStruct((share, C), f32),
        ),
        in_specs=[any_] * 3,
        out_specs=[any_] * 3,
        scratch_shapes=[
            vm((share, full_rows), bf16),
            vm((share, full_rows), bf16),
            vm((share, full_rows), f32),
            vm((2, groups, depth, 128), bf16),
            vm((3, share, C), f32),
            vm((share, C), f32),
        ]
        + [dma((parts,))] * 3
        + [dma((3,))],
        compiler_params=pltpu.CompilerParams(vmem_limit_bytes=56 * 1024 * 1024),
        name="finish",
    )(grad_in, d_sum, totals)


def solution(mesh):
    return jax.shard_map(
        local,
        mesh=mesh,
        in_specs=(
            P("head", "tile"),
            P("head", "tile"),
            P(None, "head", None),
            P("head", None),
            P(None, "tile"),
            P("tile", None, None),
        ),
        out_specs=(P("head", "tile"), P(None, "head", None), P("head", None)),
        check_vma=False,
    )
```

```python
import functools
import math

import jax
import jax.numpy as jnp
from jax import lax
from jax.experimental import pallas as pl
from jax.experimental.pallas import tpu as pltpu
from jax.sharding import PartitionSpec as P

C = 256
HEADS = 8
NBR = 9
MARGIN = 64
BLOCK = 2 * MARGIN
WINDOW = 2 * BLOCK
CHUNK = 2 * BLOCK
NEVER = -1.0e30
SLOTS = 4

NN = (((1,), (0,)), ((), ()))
NT = (((1,), (1,)), ((), ()))


def mm(a, b, dims=NN):
    return lax.dot_general(a, b, dims, preferred_element_type=jnp.float32)


def on_mesh(tile, head):
    return {"tile": tile, "head": head}


def greet(peers):
    barrier = pltpu.get_barrier_semaphore()
    for peer in peers:
        pl.semaphore_signal(barrier, inc=1, device_id=peer, device_id_type=pl.DeviceIdType.MESH)
    pl.semaphore_wait(barrier, len(peers))


def remote(src, dst, send_sem, recv_sem, peer):
    return pltpu.make_async_remote_copy(
        src_ref=src,
        dst_ref=dst,
        send_sem=send_sem,
        recv_sem=recv_sem,
        device_id=peer,
        device_id_type=pl.DeviceIdType.MESH,
    )


def send(*args):
    copy = remote(*args)
    copy.start()
    return copy


def attention_body(
    groups, heads, share, border, rows, grad_scale,
    tokens, grad_in, w_qkv, w_out, neighbors_in, send_rows_in,
    d_out, totals_out,
    tok, xr, yr, wr, wkd, wvp, wt, chosen, mine, bias_s, twice,
    k_s, v_s, kt_s, vt_s, qaug, qdiag, gdiag, e_s, p_s, ds_s,
    gk_s, gv_s, att_s, gq_s, dw, dwo, pr, fr, s1, rs, totals,
    dout, bk, db, answers, result, br, neighbors, send_rows,
    local_sem, w_send, w_recv, wf_send, wf_recv, xp_send, xp_recv, yp_send, yp_recv,
    x_send, x_recv, y_send, y_recv, e_send, e_recv, ef_send, ef_recv,
    d_send, d_recv, b_send, b_recv, a_send, a_recv, p_send, p_recv, f_send, f_recv,
    r_send, r_recv, g_send, g_recv, out_sem,
):
    head_dim = C // HEADS
    wide_head = 2 * head_dim
    pairs = HEADS // 2
    scale = 1.0 / math.sqrt(head_dim)
    scale2 = scale / math.log(2.0)
    near = rows + BLOCK
    keys = near + 3 * border
    wide = WINDOW + 3 * border
    tiles = wide // BLOCK
    full_rows = rows * heads
    chunks = rows // CHUNK
    bf16, f32 = jnp.bfloat16, jnp.float32
    tile, me = lax.axis_index("tile"), lax.axis_index("head")
    offsets = (1, groups - 1, groups // 2)
    partner = (me // 2) * 2 + 1 - me % 2
    steps = range(2, heads, 2)
    others = [(me + k) % heads for k in range(1, heads)]
    peers = [(tile + k) % groups for k in range(1, groups)]

    def rows_of(index):
        return pl.ds(pl.multiple_of(index * share, share), share)

    def lanes(start, size):
        return pl.ds(pl.multiple_of(start, BLOCK), size)

    greet(
        [on_mesh(tile, to) for to in others]
        + [on_mesh(to, me) for to in peers]
        + [on_mesh((tile + offset) % groups, to) for offset in offsets for to in others]
    )

    locals_ = [pltpu.make_async_copy(tokens, tok, local_sem.at[0])]
    pairs_of = ((tokens, xr), (grad_in, yr))
    own = lanes(me * rows, rows)
    after = lanes(((me + 1) % heads) * rows, BLOCK)
    for i, (src, dst) in enumerate(pairs_of):
        locals_.append(pltpu.make_async_copy(src.at[:, own], dst.at[rows_of(me), 0:rows], local_sem.at[1 + 2 * i]))
        locals_.append(
            pltpu.make_async_copy(src.at[:, after], dst.at[rows_of(me), rows:near], local_sem.at[2 + 2 * i])
        )
    locals_.append(pltpu.make_async_copy(w_qkv, wr.at[0:3, rows_of(me), :], local_sem.at[5]))
    locals_.append(pltpu.make_async_copy(w_out, wr.at[3, rows_of(me), :], local_sem.at[6]))
    locals_.append(pltpu.make_async_copy(neighbors_in, neighbors, local_sem.at[7]))
    rows_copy = pltpu.make_async_copy(send_rows_in, send_rows, local_sem.at[8])
    rows_copy.start()
    for copy in locals_:
        copy.start()

    w_copies = []
    for i, to in enumerate([(me + k) % heads for k in steps] + [partner]):
        w_copies.append(
            [
                send(w_qkv, wr.at[0:3, rows_of(me), :], w_send.at[0, i], w_recv.at[0, i], on_mesh(tile, to)),
                send(w_out, wr.at[3, rows_of(me), :], w_send.at[1, i], w_recv.at[1, i], on_mesh(tile, to)),
            ]
        )
    def piece(c):
        return lanes(BLOCK + c * CHUNK, CHUNK)

    def start_chunk(c):
        first = BLOCK + c * CHUNK
        for i, to in enumerate(others):
            for src, dst, ss, rr in ((tokens, xr, x_send, x_recv), (grad_in, yr, y_send, y_recv)):
                for at in (first, first + BLOCK):
                    frm = (to * rows + at) % full_rows
                    send(
                        src.at[:, lanes(frm, BLOCK)], dst.at[rows_of(me), lanes(at, BLOCK)],
                        ss.at[i, c], rr.at[i, c], on_mesh(tile, to),
                    )

    def chunk_copies(c):
        copies = []
        for i, to in enumerate(others):
            for src, dst, ss, rr in ((tokens, xr, x_send, x_recv), (grad_in, yr, y_send, y_recv)):
                copies.append(
                    remote(
                        src.at[:, 0:CHUNK], dst.at[rows_of(me), piece(c)],
                        ss.at[i, c], rr.at[i, c], on_mesh(tile, to),
                    )
                )
        return copies

    rows_copy.wait()
    flat = send_rows[...]

    def choose(i, carry):
        ids = lax.broadcasted_iota(jnp.int32, (CHUNK, 3 * border), 0) + i * CHUNK
        at = pl.ds(pl.multiple_of(i * CHUNK, CHUNK), CHUNK)
        chosen[at, :] = jnp.where(ids == flat, 1.0, 0.0).astype(bf16)
        return carry

    lax.fori_loop(0, full_rows // CHUNK, choose, 0)
    locals_[0].wait()
    mine[...] = mm(tok[...], chosen[...]).astype(bf16)
    e_copies = []
    for p in range(3):
        there = (tile + offsets[p]) % groups
        cols = slice(near + p * border, near + (p + 1) * border)
        for i, to in enumerate([(me + k) % heads for k in steps] + [me, partner]):
            e_copies.append(
                send(
                    mine.at[:, p * border : (p + 1) * border], xr.at[rows_of(me), cols],
                    e_send.at[p, i], e_recv.at[p, i], on_mesh(there, to),
                )
            )

    moving = []
    for i, to in enumerate(others):
        for src, dst, ss, rr in ((tokens, xr, xp_send, xp_recv), (grad_in, yr, yp_send, yp_recv)):
            moving.append(
                send(src.at[:, lanes(to * rows, BLOCK)], dst.at[rows_of(me), 0:BLOCK], ss.at[i], rr.at[i], on_mesh(tile, to))
            )

    start_chunk(0)

    locals_[7].wait()
    def mask(b, carry):
        start = pl.multiple_of(b * BLOCK, BLOCK)
        here = me * rows + start
        one = neighbors[:, lanes(here, BLOCK)]
        two = neighbors[:, lanes((here + BLOCK) % full_rows, BLOCK)]
        ring = jnp.concatenate([one[:, MARGIN:], two[:, :MARGIN]], axis=1)
        along = ring - me * rows
        along = jnp.where(along < 0, along + full_rows, along)
        picks = jnp.where(ring < full_rows, along - start, ring - full_rows + WINDOW)
        for t in range(tiles):
            ids = lax.broadcasted_iota(jnp.int32, (BLOCK, BLOCK), 0) + t * BLOCK
            count = jnp.zeros((BLOCK, BLOCK), f32)
            for j in range(NBR):
                count = count + jnp.where(ids == picks[j : j + 1, :], 1.0, 0.0)
            bias = jnp.where(count > 0.0, jnp.log2(jnp.maximum(count, 1.0)), NEVER)
            bias_s[pl.ds(pl.multiple_of(b * wide + t * BLOCK, BLOCK), BLOCK), :] = bias.astype(bf16)
        return carry

    lax.fori_loop(0, rows // BLOCK, mask, 0)
    qaug[...] = jnp.zeros_like(qaug)
    qdiag[...] = jnp.zeros_like(qdiag)
    gdiag[...] = jnp.zeros_like(gdiag)
    gk_s[...] = jnp.zeros_like(gk_s)
    gv_s[...] = jnp.zeros_like(gv_s)
    dw[...] = jnp.zeros_like(dw)
    att_s[...] = jnp.zeros_like(att_s)
    gq_s[...] = jnp.zeros_like(gq_s)
    diag = jnp.where(
        lax.broadcasted_iota(jnp.int32, (BLOCK, BLOCK), 0) == lax.broadcasted_iota(jnp.int32, (BLOCK, BLOCK), 1), 1.0, 0.0
    ).astype(bf16)
    twice[:, :BLOCK] = diag
    twice[:, BLOCK:] = diag
    wvp[...] = jnp.zeros_like(wvp)

    last = []
    for i, k in enumerate(steps):
        for copy in w_copies[i]:
            copy.wait()
        block_ref = wr.at[:, rows_of((me + heads - k) % heads), :]
        last.append(send(block_ref, block_ref, wf_send.at[i], wf_recv.at[i], on_mesh(tile, partner)))
    for copy in w_copies[len(steps)]:
        copy.wait()
    for copy in e_copies:
        copy.wait()
    for i, k in enumerate(steps):
        block_ref = xr.at[rows_of((me + heads - k) % heads), near:keys]
        last.append(send(block_ref, block_ref, ef_send.at[i], ef_recv.at[i], on_mesh(tile, partner)))
    for copy in locals_[1:7]:
        copy.wait()
    for i in range(len(steps)):
        last[i].wait()
    for t in range(3):
        wt[t] = wr[t].T
    for pair in range(pairs):
        chan = slice(pair * wide_head, (pair + 1) * wide_head)
        base = pair * 2 * wide_head
        wkd[base : base + wide_head, :] = wr[1, chan, :]
        wkd[base + wide_head : base + 2 * wide_head, :] = wr[1, chan, :]
        wvp[base : base + wide_head, :] = wr[2, chan, :]

    lane_id = lax.broadcasted_iota(jnp.int32, (1, 2 * C), 1) % (2 * wide_head)
    ones = jnp.where((lane_id >= wide_head) & (lane_id < wide_head + 3), 1.0, 0.0)

    def project(at_rows, at_cols):
        x = xr[:, at_cols]
        xt = x.T
        k_s[at_rows, :] = mm(xt, wkd[...], NT).astype(bf16)
        v_s[at_rows, :] = (mm(xt, wvp[...], NT) + ones).astype(bf16)
        kt_s[:, at_cols] = mm(wr[1], x).astype(bf16)
        vt_s[:, at_cols] = mm(wr[2], x).astype(bf16)

    for copy in moving:
        copy.wait()
    project(slice(0, BLOCK), slice(0, BLOCK))
    for i in range(len(steps)):
        last[len(steps) + i].wait()
    project(slice(near, keys), slice(near, keys))

    def shifted(ref, cols, size):
        return pltpu.roll(ref[:, lanes(cols, size + BLOCK)], size + MARGIN, 1)[:, :size].astype(bf16)

    def query_terms(cols, size):
        here = lanes(cols, size)
        gq, att = shifted(gq_s, cols, size), shifted(att_s, cols, size)
        dw[:, :C] += mm(gq, xr[:, here], NT)
        dw[:, C : 2 * C] += mm(att, yr[:, here], NT)
        return gq

    def key_terms(cols, size):
        here = lanes(cols, size)
        gk = (gk_s[:, here] * scale).astype(bf16)
        gv = gv_s[:, here].astype(bf16)
        dw[:, 2 * C : 3 * C] += mm(gk, xr[:, here], NT)
        dw[:, 3 * C : 4 * C] += mm(gv, xr[:, here], NT)
        return gk, gv

    def input_terms(cols, size, gq, gk, gv):
        here = lanes(cols, size)
        d = mm(wt[0], gq) + mm(wt[1], gk) + mm(wt[2], gv)
        dout[:, here] = d.astype(bf16)
        bk[me, :, here] = dout[rows_of(me), here]

    def gradients(cols, size):
        gq = query_terms(cols, size)
        gk, gv = key_terms(cols, size)
        input_terms(cols, size, gq, gk, gv)

    def d_copies(cols, size, c):
        return [
            remote(
                dout.at[rows_of(to), lanes(cols, size)], bk.at[me, :, lanes(cols, size)],
                d_send.at[i, c], d_recv.at[i, c], on_mesh(tile, to),
            )
            for i, to in enumerate(others)
        ]

    def chunk(c, carry):
        base = pl.multiple_of(c * CHUNK, CHUNK)
        for copy in chunk_copies(c):
            copy.wait()

        @pl.when(c + 1 < chunks)
        def _():
            start_chunk(c + 1)

        @pl.when(c + 1 == chunks)
        def _():
            for before in range(chunks - 2):
                for copy in d_copies(before * CHUNK, CHUNK, before):
                    copy.start()

        project(pl.ds(pl.multiple_of(base + BLOCK, BLOCK), CHUNK), piece(c))
        gradients(jnp.maximum(c - 1, 0) * CHUNK, CHUNK)
        around = lanes(base, CHUNK + BLOCK)
        q = pltpu.roll(mm(wr[0], xr[:, around]), CHUNK + MARGIN, 1)[:, :CHUNK].astype(bf16)
        g = pltpu.roll(mm(wr[3], yr[:, around]), CHUNK + MARGIN, 1)[:, :CHUNK].astype(bf16)
        scaled = q.astype(f32) * scale2
        high = scaled.astype(bf16)
        low = (scaled - high.astype(f32)).astype(bf16)
        for half in range(2):
            cols = slice(half * BLOCK, (half + 1) * BLOCK)
            for pair in range(pairs):
                u = half * pairs + pair
                for side in range(2):
                    chan = slice((pair * 2 + side) * head_dim, (pair * 2 + side + 1) * head_dim)
                    at = slice(side * head_dim, (side + 1) * head_dim)
                    under = slice(wide_head + side * head_dim, wide_head + (side + 1) * head_dim)
                    lane = slice(side * BLOCK, (side + 1) * BLOCK)
                    qaug[u, at, lane] = high[chan, cols]
                    qaug[u, under, lane] = low[chan, cols]
                    qdiag[u, at, lane] = q[chan, cols]
                    gdiag[u, at, lane] = g[chan, cols]

        units = 2 * pairs
        total, inv, right = {}, {}, {}

        def place(u):
            half, pair = u // pairs, u % pairs
            start = pl.multiple_of(base + half * BLOCK, BLOCK)
            return start, pair, slice(pair * wide_head, (pair + 1) * wide_head)

        def part_rows(part):
            return (slice(0, WINDOW), 0) if part == 0 else (slice(WINDOW, wide), WINDOW)

        def key_rows(u, part):
            return pl.ds(place(u)[0], WINDOW) if part == 0 else slice(near, keys)

        def score(u, part):
            pair = u % pairs
            at, row = part_rows(part)
            left = jnp.concatenate(
                [
                    k_s[key_rows(u, part), pair * BLOCK : (pair + 1) * BLOCK],
                    bias_s[pl.ds(pl.multiple_of((c * 2 + u // pairs) * wide + row, BLOCK), at.stop - row), :],
                ],
                axis=1,
            )
            e = jnp.exp2(mm(left, jnp.concatenate([qaug[u], twice[...]], axis=0)))
            some = jnp.sum(e.reshape((at.stop - row) // 8, 8, 2 * BLOCK), axis=0)
            total[u] = some if part == 0 else total[u] + some
            e_s[u % SLOTS, at, :] = e

        def normal(u, part):
            if part == 0:
                inv[u] = 1.0 / jnp.sum(total[u], axis=0, keepdims=True)
            at, _ = part_rows(part)
            p = e_s[u % SLOTS, at, :] * inv[u]
            e_s[u % SLOTS, at, :] = p
            p_s[u % 3, at, :] = p.astype(bf16)

        def spans(u):
            return (lanes(place(u)[0], WINDOW), slice(0, WINDOW)), (slice(near, keys), slice(WINDOW, wide))

        def attend(u):
            start, pair, chan = place(u)
            att = jnp.zeros((wide_head, 2 * BLOCK), f32)
            for span, at in spans(u):
                att = att + mm(vt_s[chan, span], p_s[u % 3, at, :])
            gd = gdiag[u]
            mean = -jnp.sum(att * gd.astype(f32), axis=0, keepdims=True)
            m0 = mean.astype(bf16).astype(f32)
            m1 = (mean - m0).astype(bf16).astype(f32)
            m2 = mean - m0 - m1
            ids = lax.broadcasted_iota(jnp.int32, (16, 2 * BLOCK), 0)
            rows3 = jnp.where(ids == 0, m0, jnp.where(ids == 1, m1, jnp.where(ids == 2, m2, 0.0))).astype(bf16)
            right[u] = jnp.concatenate([gd, rows3, jnp.zeros((wide_head - 16, 2 * BLOCK), bf16)], axis=0)
            cols = lanes(start + BLOCK, BLOCK)
            first = pair * wide_head
            att_s[first : first + head_dim, cols] = att[:head_dim, :BLOCK]
            att_s[first + head_dim : first + wide_head, cols] = att[head_dim:, BLOCK:]

        def value_grad(u):
            _, _, chan = place(u)
            pt = p_s[u % 3].T
            for span, at in spans(u):
                gv_s[chan, span] += mm(gdiag[u], pt[:, at])

        def dscore(u, part):
            pair = u % pairs
            at, _ = part_rows(part)
            dp = mm(v_s[key_rows(u, part), pair * BLOCK : (pair + 1) * BLOCK], right[u])
            ds_s[u % 3, at, :] = (e_s[u % SLOTS, at, :] * dp).astype(bf16)

        def query_grad(u):
            start, pair, chan = place(u)
            gq = jnp.zeros((wide_head, 2 * BLOCK), f32)
            for span, at in spans(u):
                gq = gq + mm(kt_s[chan, span], ds_s[u % 3, at, :])
            gq = gq * scale
            cols = lanes(start + BLOCK, BLOCK)
            first = pair * wide_head
            gq_s[first : first + head_dim, cols] = gq[:head_dim, :BLOCK]
            gq_s[first + head_dim : first + wide_head, cols] = gq[head_dim:, BLOCK:]

        def key_grad(u):
            _, _, chan = place(u)
            dt = ds_s[u % 3].T
            for span, at in spans(u):
                gk_s[chan, span] += mm(qdiag[u], dt[:, at])

        for i in range(units + 3):
            if 1 <= i < units + 1:
                normal(i - 1, 0)
                normal(i - 1, 1)
            if 0 <= i < units + 0:
                score(i - 0, 0)
                score(i - 0, 1)
            if 1 <= i < units + 1:
                attend(i - 1)
            if 2 <= i < units + 2:
                dscore(i - 2, 0)
                dscore(i - 2, 1)
            if 2 <= i < units + 2:
                value_grad(i - 2)
            if 3 <= i < units + 3:
                query_grad(i - 3)
            if 3 <= i < units + 3:
                key_grad(i - 3)

        return carry

    lax.fori_loop(0, chunks, chunk, 0)

    tail = d_copies((chunks - 2) * CHUNK, CHUNK, chunks - 2) + d_copies((chunks - 1) * CHUNK, CHUNK, chunks - 1) + d_copies(rows, BLOCK, chunks)
    far = slice(near, keys)
    halves = range(0, heads, 2)
    half_cols = 2 * C

    def to_partner(part):
        cols = slice(part * half_cols, (part + 1) * half_cols)
        dwo[part] = (dw[:, cols] * grad_scale).astype(bf16)
        return [
            send(
                dwo.at[part, rows_of((partner + k) % heads)], pr.at[part, i],
                p_send.at[part, i], p_recv.at[part, i], on_mesh(tile, partner),
            )
            for i, k in enumerate(halves)
        ]

    kept, f_copies, r_copies, g_copies = {}, {}, {}, {}

    def to_far(part, copies):
        cols = slice(part * half_cols, (part + 1) * half_cols)
        for copy in copies:
            copy.wait()
        f_copies[part] = []
        for i, k in enumerate(halves):
            value = dw[rows_of((me + k) % heads), cols] * grad_scale + pr[part, i].astype(f32)
            if k:
                fr[part, i - 1] = value.astype(bf16)
                f_copies[part].append(
                    send(
                        fr.at[part, i - 1], fr.at[part, len(halves) - 1 + i - 1],
                        f_send.at[part, i - 1], f_recv.at[part, i - 1], on_mesh(tile, (me + k) % heads),
                    )
                )
            else:
                kept[part] = value

    depth = s1.shape[2]
    blocks = half_cols // 128

    def to_tiles(part):
        for copy in f_copies[part]:
            copy.wait()
        total = kept[part]
        for i in range(len(halves) - 1):
            total = total + fr[part, len(halves) - 1 + i].astype(f32)
        for g in range(groups):
            row, col = (g // blocks) * depth, (g % blocks) * 128
            s1[part, g] = total[row : row + depth, col : col + 128].astype(bf16)
        r_copies[part] = [
            send(s1.at[part, to], rs.at[part, i], r_send.at[part, i], r_recv.at[part, i], on_mesh(to, me))
            for i, to in enumerate(peers)
        ]

    def from_tiles(part):
        for copy in r_copies[part]:
            copy.wait()
        total = s1[part, tile].astype(f32)
        for i in range(groups - 1):
            total = total + rs[part, i].astype(f32)
        totals[part, tile] = total.astype(bf16)
        g_copies[part] = [
            send(
                totals.at[part, tile], totals.at[part, tile],
                g_send.at[part, i], g_recv.at[part, i], on_mesh(to, me),
            )
            for i, to in enumerate(peers)
        ]

    left, size = rows - CHUNK, CHUNK + BLOCK
    gq_left = query_terms(left, size)
    first = to_partner(0)
    gk_left, gv_left = key_terms(left, size)
    gk, gv = key_terms(near, 3 * border)
    second = to_partner(1)
    to_far(0, first)
    to_far(1, second)
    input_terms(left, size, gq_left, gk_left, gv_left)
    db[...] = (mm(wt[1], gk) + mm(wt[2], gv)).astype(bf16)
    b_copies = [
        send(db.at[rows_of(to), :], br.at[i], b_send.at[i], b_recv.at[i], on_mesh(tile, to))
        for i, to in enumerate(others)
    ]
    for copy in tail:
        copy.start()
    to_tiles(0)
    to_tiles(1)
    for copy in b_copies:
        copy.wait()
    edge_sum = db[rows_of(me), :].astype(f32)
    for i in range(heads - 1):
        edge_sum = edge_sum + br[i].astype(f32)
    mine[...] = edge_sum.astype(bf16)
    a_copies = [
        send(
            mine.at[:, p * border : (p + 1) * border], answers.at[p],
            a_send.at[p], a_recv.at[p], on_mesh((tile + groups - offsets[p]) % groups, me),
        )
        for p in range(3)
    ]
    from_tiles(0)
    from_tiles(1)

    for copy in a_copies:
        copy.wait()
    for copy in tail:
        copy.wait()

    def d_wait(c, carry):
        for copy in d_copies(c * CHUNK, CHUNK, c):
            copy.wait()
        return carry

    lax.fori_loop(0, chunks - 2, d_wait, 0)
    back = jnp.concatenate([answers[p] for p in range(3)], axis=1)
    for h in range(heads):
        for i in range(rows // CHUNK):
            cols = slice(h * rows + i * CHUNK, h * rows + (i + 1) * CHUNK)
            value = bk[h, :, i * CHUNK : (i + 1) * CHUNK].astype(f32)
            value = value + mm(back, chosen[cols, :], NT)
            if i == 0:
                edge = bk[(h - 1) % heads, :, rows:near].astype(f32)
                value = value + jnp.concatenate([edge, jnp.zeros((share, CHUNK - BLOCK), f32)], axis=1)
            result[:, cols] = value.astype(bf16)
    out_copy = pltpu.make_async_copy(result, d_out, out_sem.at[0])
    out_copy.start()

    for part in range(2):
        for copy in g_copies[part]:
            copy.wait()
    totals_out[...] = totals[...]
    out_copy.wait()


def finish_body(
    grad_in, d_sum, totals_in, d_out, gqkv_to, gout_to,
    dy, summed, result, totals, gqkv_out, gout_out, in_sem, sum_sem, out_sem, small_sem,
):
    parts = in_sem.shape[0]
    width = dy.shape[1] // parts
    _, groups, depth, _ = totals.shape
    blocks = 2 * C // 128
    cols = [slice(i * width, (i + 1) * width) for i in range(parts)]
    first = pltpu.make_async_copy(totals_in, totals, small_sem.at[0])
    first.start()
    copies = []
    for i in range(parts):
        copies.append(
            (
                pltpu.make_async_copy(grad_in.at[:, cols[i]], dy.at[:, cols[i]], in_sem.at[i]),
                pltpu.make_async_copy(d_sum.at[:, cols[i]], summed.at[:, cols[i]], sum_sem.at[i]),
            )
        )
        for copy in copies[-1]:
            copy.start()
    first.wait()
    for part in range(2):
        for g in range(groups):
            row, col = (g // blocks) * depth, (g % blocks) * 128
            lane = col % C
            value = totals[part, g].astype(jnp.float32)
            if part == 0 and col >= C:
                gout_out[row : row + depth, lane : lane + 128] = value
            else:
                gqkv_out[part + col // C, row : row + depth, lane : lane + 128] = value
    outs = [
        pltpu.make_async_copy(gqkv_out, gqkv_to, small_sem.at[1]),
        pltpu.make_async_copy(gout_out, gout_to, small_sem.at[2]),
    ]
    for copy in outs:
        copy.start()
    for i in range(parts):
        for copy in copies[i]:
            copy.wait()
        result[:, cols[i]] = dy[:, cols[i]].astype(jnp.float32) + summed[:, cols[i]].astype(jnp.float32)
        outs.append(pltpu.make_async_copy(result.at[:, cols[i]], d_out.at[:, cols[i]], out_sem.at[i]))
        outs[-1].start()
    for copy in outs:
        copy.wait()


def local(tokens, grad_in, w_qkv, w_out, neighbors, send_rows):
    groups = lax.axis_size("tile")
    heads = lax.axis_size("head")
    border = send_rows.shape[2]
    share, full_rows = tokens.shape
    rows = full_rows // heads
    near = rows + BLOCK
    keys = near + 3 * border
    wide = WINDOW + 3 * border
    bf16, f32 = jnp.bfloat16, jnp.float32
    grad_scale = 1.0 / math.sqrt(full_rows * groups)
    vm = pltpu.VMEM
    dma = pltpu.SemaphoreType.DMA
    far = (heads - 1) // 2
    others, peers = heads - 1, groups - 1
    depth = share * 2 * C // 128 // groups
    chunks = rows // CHUNK
    units = HEADS
    any_ = pl.BlockSpec(memory_space=pl.ANY)
    in_vm = pl.BlockSpec(memory_space=vm)
    d_sum, totals = pl.pallas_call(
        functools.partial(attention_body, groups, heads, share, border, rows, grad_scale),
        out_shape=(
            jax.ShapeDtypeStruct((share, full_rows), bf16),
            jax.ShapeDtypeStruct((2, groups, depth, 128), bf16),
        ),
        in_specs=[any_] * 6,
        out_specs=[any_, in_vm],
        scratch_shapes=[
            vm((share, full_rows), bf16),
            vm((C, keys), bf16),
            vm((C, near), bf16),
            vm((4, C, C), bf16),
            vm((2 * C, C), bf16),
            vm((2 * C, C), bf16),
            vm((3, C, C), bf16),
            vm((full_rows, 3 * border), bf16),
            vm((share, 3 * border), bf16),
            vm((rows // BLOCK * wide, BLOCK), bf16),
            vm((BLOCK, 2 * BLOCK), bf16),
            vm((keys, 2 * C), bf16),
            vm((keys, 2 * C), bf16),
            vm((C, keys), bf16),
            vm((C, keys), bf16),
            vm((units, BLOCK, 2 * BLOCK), bf16),
            vm((units, 2 * C // HEADS, 2 * BLOCK), bf16),
            vm((units, 2 * C // HEADS, 2 * BLOCK), bf16),
            vm((SLOTS, wide, 2 * BLOCK), f32),
            vm((3, wide, 2 * BLOCK), bf16),
            vm((3, wide, 2 * BLOCK), bf16),
            vm((C, keys), f32),
            vm((C, keys), f32),
            vm((C, near + BLOCK), f32),
            vm((C, near + BLOCK), f32),
            vm((C, 4 * C), f32),
            vm((2, C, 2 * C), bf16),
            vm((2, heads // 2, share, 2 * C), bf16),
            vm((2, 2 * far, share, 2 * C), bf16),
            vm((2, groups, depth, 128), bf16),
            vm((2, peers, depth, 128), bf16),
            vm((2, groups, depth, 128), bf16),
            vm((C, near), bf16),
            vm((heads, share, near), bf16),
            vm((C, 3 * border), bf16),
            vm((3, share, border), bf16),
            vm((share, full_rows), bf16),
            vm((heads - 1, share, 3 * border), bf16),
            vm((NBR, full_rows), jnp.int32),
            vm((1, 3 * border), jnp.int32),
        ]
        + [dma((9,))]
        + [dma((2, far + 1))] * 2
        + [dma((far,))] * 2
        + [dma((others,))] * 4
        + [dma((others, chunks))] * 4
        + [dma((3, far + 2))] * 2
        + [dma((far,))] * 2
        + [dma((others, chunks + 1))] * 2
        + [dma((others,))] * 2
        + [dma((3,))] * 2
        + [dma((2, heads // 2))] * 2
        + [dma((2, far))] * 2
        + [dma((2, peers))] * 4
        + [dma((1,))],
        compiler_params=pltpu.CompilerParams(
            collective_id=0, has_side_effects=True, vmem_limit_bytes=56 * 1024 * 1024
        ),
        name="attend",
    )(tokens, grad_in, w_qkv, w_out, neighbors, send_rows.reshape(1, -1))
    parts = 4
    return pl.pallas_call(
        finish_body,
        out_shape=(
            jax.ShapeDtypeStruct((share, full_rows), f32),
            jax.ShapeDtypeStruct((3, share, C), f32),
            jax.ShapeDtypeStruct((share, C), f32),
        ),
        in_specs=[any_] * 3,
        out_specs=[any_] * 3,
        scratch_shapes=[
            vm((share, full_rows), bf16),
            vm((share, full_rows), bf16),
            vm((share, full_rows), f32),
            vm((2, groups, depth, 128), bf16),
            vm((3, share, C), f32),
            vm((share, C), f32),
        ]
        + [dma((parts,))] * 3
        + [dma((3,))],
        compiler_params=pltpu.CompilerParams(vmem_limit_bytes=56 * 1024 * 1024),
        name="finish",
    )(grad_in, d_sum, totals)


def solution(mesh):
    return jax.shard_map(
        local,
        mesh=mesh,
        in_specs=(
            P("head", "tile"),
            P("head", "tile"),
            P(None, "head", None),
            P("head", None),
            P(None, "tile"),
            P("tile", None, None),
        ),
        out_specs=(P("head", "tile"), P(None, "head", None), P("head", None)),
        check_vma=False,
    )
```
